32 devices in a mesh: jobs: 2 (over y), gr: 4 (over x, core), gc: 4 (over z).
Axes of the slice: x: 2, y: 2, z: 4, core: 2. Of those that a mesh axis runs over, the one named last changes fastest.
Arguments:
- pair: bfloat16 [160, 80, 128], P(('jobs', 'gr'), 'gc'), parts along dimension 0, may hold values from -6 to 6
- mask: int32 [160], P('jobs'), parts along dimension 0, may hold values 0 or 1
- chain_ids: int32 [160], P('jobs'), parts along dimension 0, may hold values from 0 to 3, never falling along the last dimension, each value on 1 to 40 neighbouring positions
- attn_in: bfloat16 [2, 128, 512], replicated, may hold values from -0.5 to 0.5
- attn_out: bfloat16 [2, 128, 128], replicated, may hold values from -0.5 to 0.5
- bias_weight: bfloat16 [2, 128, 4], replicated, may hold values from -16 to 16
- chain_bias: float32 [2, 4], replicated, may hold values from -6 to 6
- trans_up: bfloat16 [128, 512], replicated, may hold values from -0.5 to 0.5
- trans_down: bfloat16 [512, 128], replicated, may hold values from -0.25 to 0.25
Outputs:
- result: bfloat16 [160, 80, 128], P(('jobs', 'gr'), 'gc'), parts along dimension 0
The draws below stay inside these ranges and needn't reach their ends.
There are 2 independent parts, one for each index of `jobs`. The reference program is written for one: setup_inputs(seed, part) draws one part's arguments, and reference() takes and returns one part's arrays. A program takes and returns all parts, laid end to end along the dimension named above; an argument that names none is the same for every part. Nothing has to cross between parts.
All inputs are finite; a program needn't handle non-finite values.
Results may differ from the reference program's by a relative error of at most 0.008.
The reference program's roundings to bfloat16 on the way count: a program that leaves them out, or rounds other values in their place, can miss the bound.
Values may be sent and summed in bfloat16 or wider, within the bound.
No kernel may reach another device: no remote copies, remote signals or barrier semaphores. Data moves between devices by JAX's collectives and lax.ppermute only.
A program may use at most 64 MiB of HBM per device.

```python
import math
import jax
import jax.numpy as jnp
import numpy as np
from jax import lax

C = 128
HEADS = 4
FF = 512
TOKENS = 80
HEAD_DIM = 32


root_three = 1.7320508


def draw_bias_weight(key, part):
    base = jax.random.uniform(key, (2, C, HEADS), jnp.float32, -root_three, root_three)
    base = base / jnp.sqrt(jnp.float32(C))
    return base.astype(jnp.bfloat16)


def set_ends(entries, rng, low, largest):
    longest = entries.shape.index(max(entries.shape))
    spots = []
    for shift in (0, 1):
        where = [jax.random.randint(jax.random.fold_in(rng, axis), (), 0, length) for axis, length in enumerate(entries.shape)]
        where[longest] = (where[longest] + shift) % entries.shape[longest]
        spots.append(tuple(where))
    return entries.at[spots[0]].set(low).at[spots[1]].set(largest)


def steps_of(rng, shape, pieces, least, high):
    def one(axis_at, parts):
        steps = jax.random.uniform(jax.random.fold_in(jax.random.fold_in(rng, 6), axis_at), (parts,), jnp.float32, least / len(pieces), high / len(pieces))
        return jnp.repeat(jnp.exp(steps), shape[axis_at] // parts).reshape((-1,) + (1,) * (len(shape) - axis_at - 1))

    level = one(*pieces[0])
    for cut in pieces[1:]:
        level = level * one(*cut)
    return level


def length_profile(amount, total, bound, lean):
    weights = [(1 << 20) // math.isqrt(grade ** lean) + 1 for grade in range(2, amount + 1)]
    surplus, holding = total - bound - (amount - 1), [1] * (amount - 1)
    while surplus > 0:
        free = [i for i in range(amount - 1) if holding[i] < bound]
        whole, remaining = sum([weights[i] for i in free]), surplus
        for i in free:
            extra = min(bound - holding[i], max(1, remaining * weights[i] // whole), surplus)
            holding[i] = holding[i] + extra
            surplus = surplus - extra
    return np.array([bound] + holding)


def uneven(own_key, number_of, total, bound, lean):
    if number_of == 2:
        one = jax.random.randint(own_key, (), max(1, total - bound), min(bound, total - 1) + 1)
        return jnp.stack([one, total - one])
    tallies = jnp.asarray(length_profile(number_of, total, bound, lean), jnp.int32)
    pairs = (number_of - 1) // 2
    source_of, receiver = tallies[1:1 + 2 * pairs:2], tallies[2:2 + 2 * pairs:2]
    slack = jnp.minimum(source_of - 1, bound - receiver)
    moved = jax.random.randint(jax.random.fold_in(own_key, 1), (pairs,), 0, 1 << 20) % (slack + 1)
    tallies = tallies.at[1:1 + 2 * pairs:2].set(source_of - moved).at[2:2 + 2 * pairs:2].set(receiver + moved)
    return tallies[jax.random.permutation(jax.random.fold_in(own_key, 2), number_of)]


def centred(key, dims, deviation, reach, cuts=(), held_as=jnp.bfloat16):
    entries = jax.random.normal(key, dims, jnp.float32) * deviation
    if len(cuts) > 0:
        entries = steps_of(key, dims, cuts, -0.22, 0.18) * entries
    return jnp.clip(entries, min=-reach, max=reach).astype(held_as)


def setup_inputs(seed: int = 0, part: int = 0) -> dict:
    streams_of = jax.random.split(jax.random.key(seed), 10)
    part_keys = jax.random.split(jax.random.fold_in(streams_of[9], part), 10)
    return {
        "pair": centred(part_keys[0], (TOKENS, TOKENS, C), 1.0, 6.0, ((0, 4), (1, 4))),
        "mask": set_ends((jax.random.randint(part_keys[1], (TOKENS,), 0, 8) < 7).astype(jnp.int32), jax.random.fold_in(part_keys[1], 1), 0, 1),
        "chain_ids": jnp.searchsorted(jnp.cumsum(uneven(part_keys[2], 4, TOKENS, TOKENS // 2, 0)), jnp.arange(TOKENS), side="right").astype(jnp.int32),
        "attn_in": centred(streams_of[3], (2, C, 4 * C), C ** -0.5, 0.5),
        "attn_out": centred(streams_of[4], (2, C, C), C ** -0.5, 0.5),
        "bias_weight": draw_bias_weight(jax.random.fold_in(streams_of[9], 71), part),
        "chain_bias": centred(streams_of[6], (2, HEADS), 1.5, 6.0, (), jnp.float32),
        "trans_up": centred(streams_of[7], (C, FF), C ** -0.5, 0.5),
        "trans_down": centred(streams_of[8], (FF, C), FF ** -0.5, 0.25),
    }


def layer_norm(values):
    floats = values.astype(jnp.float32)
    center = lax.optimization_barrier(jnp.mean(floats, axis=-1, keepdims=True))
    spread = lax.optimization_barrier(jnp.mean((floats - center) ** 2, axis=-1, keepdims=True))
    return ((floats - center) * lax.rsqrt(spread + 1e-05)).astype(jnp.bfloat16)

def starting(pair, in_w, out_w, bias_w, chain_w, chain_ids, mask):
    normed = layer_norm(pair)
    flat = normed.reshape(-1, C)
    proj = jnp.dot(flat, in_w, preferred_element_type=jnp.float32).astype(jnp.bfloat16)
    proj = proj.reshape(TOKENS, TOKENS, 4 * C)
    same = (chain_ids[:, None] == chain_ids[None, :]).astype(jnp.float32)
    bias = jnp.dot(flat, bias_w, preferred_element_type=jnp.float32).reshape(TOKENS, TOKENS, HEADS)
    bias = bias + chain_w[None, None, :] * same[:, :, None]
    bias = jnp.transpose(bias, (2, 0, 1))
    maskadd = jnp.where(mask > 0, 0.0, -1000000000.0).astype(jnp.float32)
    scale = HEAD_DIM ** (-0.5)

    def one_row(piece):
        query = piece[:, 0:C].reshape(TOKENS, HEADS, HEAD_DIM).astype(jnp.float32)
        keys = piece[:, C:2 * C].reshape(TOKENS, HEADS, HEAD_DIM).astype(jnp.float32)
        vals = piece[:, 2 * C:3 * C].reshape(TOKENS, HEADS, HEAD_DIM).astype(jnp.float32)
        gate = piece[:, 3 * C:].astype(jnp.float32)
        scores = jnp.einsum('jhd,khd->hjk', query, keys) * scale + bias + maskadd[None, None, :]
        probs = jax.nn.softmax(scores, axis=-1).astype(jnp.bfloat16)
        mixed = jnp.einsum('hjk,khd->jhd', probs.astype(jnp.float32), vals).reshape(TOKENS, C)
        return (jax.nn.sigmoid(gate) * mixed).astype(jnp.bfloat16)
    gated = lax.map(one_row, proj)
    update = jnp.dot(gated.reshape(-1, C), out_w, preferred_element_type=jnp.float32).reshape(TOKENS, TOKENS, C)
    return (pair.astype(jnp.float32) + update).astype(jnp.bfloat16)

def reference(pair, mask, chain_ids, attn_in, attn_out, bias_weight, chain_bias, trans_up, trans_down):
    first = starting(pair, attn_in[0], attn_out[0], bias_weight[0], chain_bias[0], chain_ids, mask)
    normed = layer_norm(first).reshape(-1, C)
    hidden = jax.nn.relu(jnp.dot(normed, trans_up, preferred_element_type=jnp.float32)).astype(jnp.bfloat16)
    update = jnp.dot(hidden, trans_down, preferred_element_type=jnp.float32).reshape(TOKENS, TOKENS, C)
    second = (first.astype(jnp.float32) + update).astype(jnp.bfloat16)
    flipped = jnp.transpose(second, (1, 0, 2))
    ending = starting(flipped, attn_in[1], attn_out[1], bias_weight[1], chain_bias[1], chain_ids, mask)
    return jnp.transpose(ending, (1, 0, 2))
```

```python
import functools

import jax
import jax.numpy as jnp
from jax import lax
from jax.experimental import pallas as pl
from jax.experimental.pallas import tpu as pltpu
from jax.sharding import PartitionSpec as P

BF = jnp.bfloat16
F32 = jnp.float32


def layer_norm(values):
    floats = values.astype(F32)
    center = jnp.mean(floats, axis=-1, keepdims=True)
    spread = jnp.mean((floats - center) ** 2, axis=-1, keepdims=True)
    return ((floats - center) * lax.rsqrt(spread + 1e-05)).astype(BF)


def bias_terms(normed, weight, offset, chain_left, chain_right):
    first, second, width = normed.shape
    heads = weight.shape[1]
    terms = jnp.dot(normed.reshape(-1, width), weight, preferred_element_type=F32)
    same = (chain_left[:, None] == chain_right[None, :]).astype(F32)
    return terms.reshape(first, second, heads) + offset[None, None, :] * same[:, :, None]


def attention(rows, normed, in_w, out_w, bias_full, maskadd):
    count, length, width = rows.shape
    heads = bias_full.shape[0]
    head_width = width // heads
    scale = head_width ** (-0.5)
    proj = jnp.dot(normed.reshape(-1, width), in_w, preferred_element_type=F32)
    proj = proj.astype(BF).reshape(count, length, 4 * width)

    def one_row(piece):
        query = piece[:, 0:width].reshape(length, heads, head_width)
        keys = piece[:, width : 2 * width].reshape(length, heads, head_width)
        vals = piece[:, 2 * width : 3 * width].reshape(length, heads, head_width)
        gate = piece[:, 3 * width :].astype(F32)
        scores = jnp.einsum("jhd,khd->hjk", query, keys, preferred_element_type=F32) * scale
        scores = scores + bias_full + maskadd[None, None, :]
        probs = jax.nn.softmax(scores, axis=-1).astype(BF)
        mixed = jnp.einsum("hjk,khd->jhd", probs, vals, preferred_element_type=F32)
        return (jax.nn.sigmoid(gate) * mixed.reshape(length, width)).astype(BF)

    gated = lax.map(one_row, proj)
    update = jnp.dot(gated.reshape(-1, width), out_w, preferred_element_type=F32)
    return (rows.astype(F32) + update.reshape(rows.shape)).astype(BF)


def transition(rows, trans_up, trans_down):
    width = rows.shape[-1]
    normed = layer_norm(rows).reshape(-1, width)
    hidden = jax.nn.relu(jnp.dot(normed, trans_up, preferred_element_type=F32)).astype(BF)
    update = jnp.dot(hidden, trans_down, preferred_element_type=F32)
    return (rows.astype(F32) + update.reshape(rows.shape)).astype(BF)


def plain_device(
    pair, mask, chain_ids, attn_in, attn_out, bias_weight, chain_bias, trans_up, trans_down
):
    across = lax.axis_size("gc")
    rows = lax.all_to_all(pair, "gc", split_axis=0, concat_axis=1, tiled=True)
    count = rows.shape[0]
    first_row = (lax.axis_index("gr") * across + lax.axis_index("gc")) * count
    maskadd = jnp.where(mask > 0, 0.0, -1000000000.0).astype(F32)
    own_chain = lax.dynamic_slice_in_dim(chain_ids, first_row, count)
    normed = layer_norm(rows)
    start_part = bias_terms(normed, bias_weight[0], chain_bias[0], own_chain, chain_ids)
    start_full = lax.all_gather(
        jnp.transpose(start_part, (2, 0, 1)), ("gr", "gc"), axis=1, tiled=True
    )
    rows = attention(rows, normed, attn_in[0], attn_out[0], start_full, maskadd)
    tile = lax.all_to_all(rows, "gc", split_axis=1, concat_axis=0, tiled=True)
    tile = transition(tile, trans_up, trans_down)
    tile_rows, tile_cols = (tile.shape[0], tile.shape[1])
    chain_rows = lax.dynamic_slice_in_dim(chain_ids, lax.axis_index("gr") * tile_rows, tile_rows)
    chain_cols = lax.dynamic_slice_in_dim(chain_ids, lax.axis_index("gc") * tile_cols, tile_cols)
    end_part = bias_terms(layer_norm(tile), bias_weight[1], chain_bias[1], chain_rows, chain_cols)
    end_part = lax.all_gather(jnp.transpose(end_part, (2, 1, 0)), "gc", axis=1, tiled=True)
    end_full = lax.all_gather(end_part, "gr", axis=2, tiled=True)
    columns = lax.all_to_all(
        jnp.transpose(tile, (1, 0, 2)), "gr", split_axis=0, concat_axis=1, tiled=True
    )
    columns = attention(columns, layer_norm(columns), attn_in[1], attn_out[1], end_full, maskadd)
    returned = lax.all_to_all(columns, "gr", split_axis=1, concat_axis=0, tiled=True)
    return jnp.transpose(returned, (1, 0, 2))


def norm32(x):
    center = jnp.mean(x, axis=-1, keepdims=True)
    off = x - center
    spread = jnp.mean(off * off, axis=-1, keepdims=True)
    return (off * lax.rsqrt(spread + 1e-05)).astype(BF)


def tile_bias(normed, wrep, left, right, chain_w, span):
    count, _, width = normed.shape
    lanes = wrep.shape[1]
    place = lax.broadcasted_iota(jnp.int32, (width, lanes), 1) % span
    zero = jnp.zeros((width, lanes), BF)
    spread = jnp.concatenate([jnp.where(place == j, wrep, zero) for j in range(count)], axis=0)
    tokens = jnp.concatenate([normed[j] for j in range(count)], axis=1)
    terms = jnp.dot(tokens, spread, preferred_element_type=F32)
    return terms + jnp.where(left == right, chain_w, 0.0)


def first_bias_kernel(span, x_ref, wrep_ref, left_ref, right_ref, chain_ref, o_ref, pad):
    nb, nt, _ = x_ref.shape
    pad[...] = jnp.zeros_like(pad)
    pad[:, 0:nt, :] = x_ref[...].astype(F32)
    terms = tile_bias(
        norm32(pad[...]), wrep_ref[...], left_ref[...], right_ref[...], chain_ref[...], span
    )
    o_ref[...] = terms[0:nt]


def attend(spin, heads, span, chunks, bias_refs, mask_ref, in_ref, out_ref, own, gather, table):
    nb, nt, width = chunks[0].shape
    pieces = len(chunks)
    length = pieces * nt
    scale = (width // heads) ** (-0.5)
    own[...] = jnp.zeros_like(own)
    own[:, 0:nt, :] = chunks[0][...].astype(F32)
    for k in range(pieces):
        gather[:, k * nt : (k + 1) * nt, :] = chunks[k][...].astype(F32)
    for slot in range(pieces):
        for k in range(pieces):

            @pl.when(spin == (slot ^ k))
            def _():
                table[k * nt : (k + 1) * nt, :] = bias_refs[slot][...]

    weights = in_ref[...]
    mine = norm32(own[...].reshape(nb * span, width))
    w_query = jnp.concatenate([weights[:, 0:width], weights[:, 3 * width :]], axis=1)
    ask = jnp.dot(mine, w_query, preferred_element_type=F32).astype(BF)
    query, gate = ask[:, 0:width], ask[:, width:].astype(F32)
    everyone = norm32(gather[...].reshape(nb * length, width))
    both = jnp.dot(
        everyone, weights[:, width : 3 * width], preferred_element_type=F32
    ).astype(BF)
    keys, vals = both[:, 0:width], both[:, width:]
    head_of = lax.broadcasted_iota(jnp.int32, (span, width), 1) // (width // heads)
    bias = table[...]
    away = mask_ref[...]
    mixed = []
    for b in range(nb):
        q = query[b * span : (b + 1) * span]
        wide = jnp.concatenate(
            [jnp.where(head_of == h, q, jnp.zeros_like(q)) for h in range(heads)], axis=0
        )
        k = keys[b * length : (b + 1) * length]
        v = vals[b * length : (b + 1) * length]
        s = lax.dot_general(k, wide, (((1,), (1,)), ((), ())), preferred_element_type=F32)
        s = s * scale + bias + away
        top = jnp.max(s, axis=0, keepdims=True)
        e = jnp.exp(s - top)
        p = (e * (1.0 / jnp.sum(e, axis=0, keepdims=True))).astype(BF)
        o = lax.dot_general(p, v, (((0,), (0,)), ((), ())), preferred_element_type=F32)
        got = jnp.zeros((span, width), F32)
        for h in range(heads):
            got = jnp.where(head_of == h, o[h * span : (h + 1) * span], got)
        mixed.append(got)
    mixed = jnp.concatenate(mixed, axis=0)
    gated = (jax.nn.sigmoid(gate) * mixed).astype(BF)
    update = jnp.dot(gated, out_ref[...], preferred_element_type=F32)
    return (own[...].reshape(nb * span, width) + update).astype(BF).astype(F32)


def first_kernel(heads, span, pieces, *refs):
    spin_ref = refs[0]
    chunks = refs[1 : 1 + pieces]
    bias_refs = refs[1 + pieces : 1 + 2 * pieces]
    (
        mask_ref, in_ref, out_ref, up_ref, down_ref, wrep_ref, left_ref, right_ref, chain_ref,
        tile_ref, bias_ref, own, gather, table, flip,
    ) = refs[1 + 2 * pieces :]
    nb, nt, width = chunks[0].shape
    first = attend(
        spin_ref[0], heads, span, chunks, bias_refs, mask_ref, in_ref, out_ref, own, gather, table
    )
    hidden = jnp.dot(norm32(first), up_ref[...], preferred_element_type=F32)
    hidden = jnp.maximum(hidden, 0.0).astype(BF)
    update = jnp.dot(hidden, down_ref[...], preferred_element_type=F32)
    second = (first + update).astype(BF).astype(F32)
    flip[...] = jnp.zeros_like(flip)
    for b in range(nb):
        flip[:, b, :] = second[b * span : b * span + nt]
    turned = flip[...]
    tile_ref[...] = turned[:, 0:nb].astype(BF)
    terms = tile_bias(
        norm32(turned), wrep_ref[...], left_ref[...], right_ref[...], chain_ref[...], span
    )
    bias_ref[...] = terms[0:nb]


def second_kernel(heads, span, pieces, *refs):
    spin_ref = refs[0]
    chunks = refs[1 : 1 + pieces]
    bias_refs = refs[1 + pieces : 1 + 2 * pieces]
    mask_ref, in_ref, out_ref, tile_ref, own, gather, table, flip = refs[1 + 2 * pieces :]
    nb, nt, width = chunks[0].shape
    last = attend(
        spin_ref[0], heads, span, chunks, bias_refs, mask_ref, in_ref, out_ref, own, gather, table
    )
    for b in range(nb):
        flip[:, b, :] = last[b * span : b * span + nt]
    tile_ref[...] = flip[...].astype(BF)


VMEM = pl.BlockSpec(memory_space=pltpu.VMEM)
SMEM = pl.BlockSpec(memory_space=pltpu.SMEM)


def layer_of(array, index):
    rest = array.shape[1:]
    return pl.BlockSpec((None, *rest), lambda i: (index,) + (0,) * len(rest))


def whole(array):
    return pl.BlockSpec(array.shape, lambda i: (0,) * array.ndim)


def swap(array, axis, k):
    size = lax.axis_size(axis)
    return lax.ppermute(array, axis, [(i, i ^ k) for i in range(size)])


def fast_device(
    span, pair, mask, chain_ids, attn_in, attn_out, bias_weight, chain_bias, trans_up, trans_down
):
    side = lax.axis_size("gc")
    nr, nc, width = pair.shape
    heads = bias_weight.shape[2]
    lanes = heads * span
    gr, gc = lax.axis_index("gr"), lax.axis_index("gc")
    spin = (gr ^ gc).astype(jnp.int32).reshape(1)
    cells = [(r, c) for r in range(side) for c in range(side)]
    params = pltpu.CompilerParams(dimension_semantics=("arbitrary",))

    chunks = [pair] + [swap(pair, "gc", k) for k in range(1, side)]

    wrep = jnp.repeat(bias_weight, span, axis=2)
    chain_lane = jnp.repeat(chain_bias, span, axis=1)[:, None, :]
    rows_chain = lax.dynamic_slice_in_dim(chain_ids, gr * nr, nr)
    cols_chain = lax.dynamic_slice_in_dim(chain_ids, gc * nc, nc)

    def as_query(ids):
        return jnp.tile(jnp.pad(ids, (0, span - ids.shape[0])), heads)[None, :]

    def as_key(ids):
        return jnp.broadcast_to(jnp.pad(ids, (0, span - ids.shape[0]))[:, None], (span, lanes))

    maskadd = jnp.where(mask > 0, 0.0, -1000000000.0).astype(F32)

    def mask_for(start, count):
        part = [lax.dynamic_slice_in_dim(maskadd, (start ^ k) * count, count) for k in range(side)]
        return jnp.broadcast_to(jnp.concatenate(part)[:, None], (side * count, lanes))

    piece = pl.pallas_call(
        functools.partial(first_bias_kernel, span),
        out_shape=jax.ShapeDtypeStruct((nc, lanes), F32),
        grid=(1,),
        in_specs=[whole(pair), layer_of(wrep, 0)]
        + [pl.BlockSpec((1, lanes), lambda i: (0, 0)), pl.BlockSpec((span, lanes), lambda i: (0, 0))]
        + [layer_of(chain_lane, 0)],
        out_specs=pl.BlockSpec((nc, lanes), lambda i: (0, 0)),
        scratch_shapes=[pltpu.VMEM((nr, span, width), F32)],
        compiler_params=params,
    )(pair, wrep, as_query(rows_chain), as_key(cols_chain), chain_lane)
    pieces = [
        lax.ppermute(piece, ("gr", "gc"), [(r * side + c, (c ^ k) * side + r) for r, c in cells])
        for k in range(side)
    ]
    args = [spin, *chunks, *pieces, mask_for(gc, nc), attn_in, attn_out, trans_up, trans_down, wrep]
    args += [as_query(cols_chain), as_key(rows_chain), chain_lane]
    specs = [SMEM] + [whole(a) for a in args[1 : 2 + 2 * side]]
    specs += [layer_of(attn_in, 0), layer_of(attn_out, 0), whole(trans_up), whole(trans_down)]
    specs += [layer_of(wrep, 1), whole(args[-3]), whole(args[-2]), layer_of(chain_lane, 1)]
    tile, piece = pl.pallas_call(
        functools.partial(first_kernel, heads, span, side),
        out_shape=(
            jax.ShapeDtypeStruct((nc, nr, width), BF),
            jax.ShapeDtypeStruct((nr, lanes), F32),
        ),
        grid=(1,),
        in_specs=specs,
        out_specs=(
            pl.BlockSpec((nc, nr, width), lambda i: (0, 0, 0)),
            pl.BlockSpec((nr, lanes), lambda i: (0, 0)),
        ),
        scratch_shapes=[
            pltpu.VMEM((nr, span, width), F32),
            pltpu.VMEM((nr, side * nc, width), F32),
            pltpu.VMEM((side * nc, lanes), F32),
            pltpu.VMEM((nc, span, width), F32),
        ],
        compiler_params=params,
    )(*args)

    chunks = [tile, swap(tile, "gr", 1)]
    for k in range(2, side, 2):
        far = swap(tile, "gr", k)
        chunks += [far, swap(far, "gr", 1)]
    pieces = [
        lax.ppermute(piece, ("gr", "gc"), [(r * side + c, c * side + (r ^ k)) for r, c in cells])
        for k in range(side)
    ]
    args = [spin, *chunks, *pieces, mask_for(gr, nr), attn_in, attn_out]
    specs = [SMEM] + [whole(a) for a in args[1 : 2 + 2 * side]]
    specs += [layer_of(attn_in, 1), layer_of(attn_out, 1)]
    return pl.pallas_call(
        functools.partial(second_kernel, heads, span, side),
        out_shape=jax.ShapeDtypeStruct((nr, nc, width), BF),
        grid=(1,),
        in_specs=specs,
        out_specs=pl.BlockSpec((nr, nc, width), lambda i: (0, 0, 0)),
        scratch_shapes=[
            pltpu.VMEM((nc, span, width), F32),
            pltpu.VMEM((nc, side * nr, width), F32),
            pltpu.VMEM((side * nr, lanes), F32),
            pltpu.VMEM((nr, nc, width), F32),
        ],
        compiler_params=params,
    )(*args)


def solution(mesh):
    shape = dict(mesh.shape)
    in_specs = (P(("jobs", "gr"), "gc", None), P("jobs"), P("jobs"), P(), P(), P(), P(), P(), P())
    out_specs = P(("jobs", "gr"), "gc", None)
    side = shape["gc"]
    square = shape["gr"] == side and side & (side - 1) == 0

    def per_device(*args):
        nr, nc, width = args[0].shape
        heads = args[5].shape[2]
        span = 128 // heads
        fits = nr == nc and nr <= span and (side * nr) % 16 == 0 and width == 128
        if square and fits:
            return fast_device(span, *args)
        return plain_device(*args)

    return jax.shard_map(
        per_device, mesh=mesh, in_specs=in_specs, out_specs=out_specs, check_vma=False
    )
```

```python
import functools

import jax
import jax.numpy as jnp
from jax import lax
from jax.experimental import pallas as pl
from jax.experimental.pallas import tpu as pltpu
from jax.sharding import PartitionSpec as P


BF = jnp.bfloat16
F32 = jnp.float32


def layer_norm(values):
    floats = values.astype(F32)
    center = jnp.mean(floats, axis=-1, keepdims=True)
    spread = jnp.mean((floats - center) ** 2, axis=-1, keepdims=True)
    return ((floats - center) * lax.rsqrt(spread + 1e-05)).astype(BF)


def bias_terms(normed, weight, offset, chain_left, chain_right):
    first, second, width = normed.shape
    heads = weight.shape[1]
    terms = jnp.dot(normed.reshape(-1, width), weight, preferred_element_type=F32)
    same = (chain_left[:, None] == chain_right[None, :]).astype(F32)
    return terms.reshape(first, second, heads) + offset[None, None, :] * same[:, :, None]


def attention(rows, normed, in_w, out_w, bias_full, maskadd):
    count, length, width = rows.shape
    heads = bias_full.shape[0]
    head_width = width // heads
    scale = head_width ** (-0.5)
    proj = jnp.dot(normed.reshape(-1, width), in_w, preferred_element_type=F32)
    proj = proj.astype(BF).reshape(count, length, 4 * width)

    def one_row(piece):
        query = piece[:, 0:width].reshape(length, heads, head_width)
        keys = piece[:, width : 2 * width].reshape(length, heads, head_width)
        vals = piece[:, 2 * width : 3 * width].reshape(length, heads, head_width)
        gate = piece[:, 3 * width :].astype(F32)
        scores = jnp.einsum("jhd,khd->hjk", query, keys, preferred_element_type=F32) * scale
        scores = scores + bias_full + maskadd[None, None, :]
        probs = jax.nn.softmax(scores, axis=-1).astype(BF)
        mixed = jnp.einsum("hjk,khd->jhd", probs, vals, preferred_element_type=F32)
        return (jax.nn.sigmoid(gate) * mixed.reshape(length, width)).astype(BF)

    gated = lax.map(one_row, proj)
    update = jnp.dot(gated.reshape(-1, width), out_w, preferred_element_type=F32)
    return (rows.astype(F32) + update.reshape(rows.shape)).astype(BF)


def transition(rows, trans_up, trans_down):
    width = rows.shape[-1]
    normed = layer_norm(rows).reshape(-1, width)
    hidden = jax.nn.relu(jnp.dot(normed, trans_up, preferred_element_type=F32)).astype(BF)
    update = jnp.dot(hidden, trans_down, preferred_element_type=F32)
    return (rows.astype(F32) + update.reshape(rows.shape)).astype(BF)


def plain_device(
    pair, mask, chain_ids, attn_in, attn_out, bias_weight, chain_bias, trans_up, trans_down
):
    across = lax.axis_size("gc")
    rows = lax.all_to_all(pair, "gc", split_axis=0, concat_axis=1, tiled=True)
    count = rows.shape[0]
    first_row = (lax.axis_index("gr") * across + lax.axis_index("gc")) * count
    maskadd = jnp.where(mask > 0, 0.0, -1000000000.0).astype(F32)
    own_chain = lax.dynamic_slice_in_dim(chain_ids, first_row, count)
    normed = layer_norm(rows)
    start_part = bias_terms(normed, bias_weight[0], chain_bias[0], own_chain, chain_ids)
    start_full = lax.all_gather(
        jnp.transpose(start_part, (2, 0, 1)), ("gr", "gc"), axis=1, tiled=True
    )
    rows = attention(rows, normed, attn_in[0], attn_out[0], start_full, maskadd)
    tile = lax.all_to_all(rows, "gc", split_axis=1, concat_axis=0, tiled=True)
    tile = transition(tile, trans_up, trans_down)
    tile_rows, tile_cols = (tile.shape[0], tile.shape[1])
    chain_rows = lax.dynamic_slice_in_dim(chain_ids, lax.axis_index("gr") * tile_rows, tile_rows)
    chain_cols = lax.dynamic_slice_in_dim(chain_ids, lax.axis_index("gc") * tile_cols, tile_cols)
    end_part = bias_terms(layer_norm(tile), bias_weight[1], chain_bias[1], chain_rows, chain_cols)
    end_part = lax.all_gather(jnp.transpose(end_part, (2, 1, 0)), "gc", axis=1, tiled=True)
    end_full = lax.all_gather(end_part, "gr", axis=2, tiled=True)
    columns = lax.all_to_all(
        jnp.transpose(tile, (1, 0, 2)), "gr", split_axis=0, concat_axis=1, tiled=True
    )
    columns = attention(columns, layer_norm(columns), attn_in[1], attn_out[1], end_full, maskadd)
    returned = lax.all_to_all(columns, "gr", split_axis=1, concat_axis=0, tiled=True)
    return jnp.transpose(returned, (1, 0, 2))


def norm32(x):
    center = jnp.mean(x, axis=-1, keepdims=True)
    off = x - center
    spread = jnp.mean(off * off, axis=-1, keepdims=True)
    return (off * lax.rsqrt(spread + 1e-05)).astype(BF)


def contract(a, b, da, db):
    return lax.dot_general(a, b, (((da,), (db,)), ((), ())), preferred_element_type=F32)


def tile_bias(normed, weight, chain, span):
    count, _, width = normed.shape
    heads = weight.shape[0]
    rep = jnp.concatenate(
        [jnp.broadcast_to(weight[h : h + 1].astype(F32), (span, width)) for h in range(heads)], axis=0
    )
    place = lax.broadcasted_iota(jnp.int32, rep.shape, 0) % span
    spread = jnp.concatenate(
        [jnp.where(place == j, rep, 0.0).astype(BF) for j in range(count)], axis=1
    )
    tokens = jnp.concatenate([normed[j] for j in range(count)], axis=1)
    return contract(tokens, spread, 1, 1) + chain


def chain_terms(ids, query_at, key_at, weights, heads, span):
    lanes = heads * span
    reach = ids.shape[1]
    lane = lax.broadcasted_iota(jnp.int32, (reach, lanes), 1) % span
    spot = lax.broadcasted_iota(jnp.int32, (reach, lanes), 0)
    left = contract(ids, (spot == lane + query_at).astype(F32).astype(BF), 1, 0)[0:1]
    row = lax.broadcasted_iota(jnp.int32, (span, reach), 0)
    col = lax.broadcasted_iota(jnp.int32, (span, reach), 1)
    every = jnp.broadcast_to(ids[0:1].astype(F32), (lanes, reach)).astype(BF)
    right = contract((col == row + key_at).astype(F32).astype(BF), every, 1, 1)
    head = lax.broadcasted_iota(jnp.int32, (span, lanes), 1) // span
    term = jnp.zeros((span, lanes), F32)
    for h in range(heads):
        term = jnp.where(head == h, weights[h], term)
    return jnp.where(left == right, term, 0.0)


def key_mask(mask, block, pieces, count, lanes):
    reach = mask.shape[1]
    every = jnp.broadcast_to(mask[0:1].astype(F32), (lanes, reach)).astype(BF)
    shape = (pieces * count, reach)
    row = lax.broadcasted_iota(jnp.int32, shape, 0)
    col = lax.broadcasted_iota(jnp.int32, shape, 1)
    want = jnp.full(shape, -1, jnp.int32)
    for k in range(pieces):
        inside = (row >= k * count) & (row < (k + 1) * count)
        want = jnp.where(inside, row - k * count + (block ^ k) * count, want)
    found = contract((col == want).astype(F32).astype(BF), every, 1, 1)
    return jnp.where(found > 0.0, 0.0, -1000000000.0)


def spread_ids(ref, reach):
    ids = ref[...].astype(F32)
    pad = jnp.zeros((1, reach - ids.shape[1]), F32)
    return jnp.broadcast_to(jnp.concatenate([ids, pad], axis=1), (8, reach)).astype(BF)


def first_bias_kernel(
    heads, span, side, pair_ref, in_ref, out_ref, up_ref, down_ref, weight_ref, ids_ref, mask_ref,
    chain_ref, o_ref, chain_out, row_mask, col_mask, own, in_out, out_out, up_out, down_out,
    pad, sems,
):
    nr, nc, _ = pair_ref.shape
    lanes = heads * span
    copies = [
        pltpu.make_async_copy(a, b, sems.at[i])
        for i, (a, b) in enumerate(
            (
                (pair_ref, own), (in_ref, in_out), (out_ref, out_out),
                (up_ref, up_out), (down_ref, down_out),
            )
        )
    ]
    for copy in copies:
        copy.start()
    gr, gc = lax.axis_index("gr"), lax.axis_index("gc")
    ids = spread_ids(ids_ref, lanes)
    here = chain_terms(ids, gr * nr, gc * nc, [chain_ref[0, h] for h in range(heads)], heads, span)
    chain_out[...] = chain_terms(
        ids, gc * nc, gr * nr, [chain_ref[1, h] for h in range(heads)], heads, span
    )
    mask = spread_ids(mask_ref, lanes)
    row_mask[...] = key_mask(mask, gc, side, nc, lanes)
    col_mask[...] = key_mask(mask, gr, side, nr, lanes)
    pad[...] = jnp.zeros_like(pad)
    copies[0].wait()
    pad[:, 0:nc, :] = own[...].astype(F32)
    o_ref[...] = tile_bias(norm32(pad[...]), weight_ref[0], here, span)[0:nc]
    for copy in copies[1:]:
        copy.wait()


def score_kernel(layer, heads, span, pieces, *refs):
    chunks = refs[0:pieces]
    in_ref, s_ref, v_ref, g_ref, base_ref, gather = refs[pieces:]
    nb, nt, width = chunks[0].shape
    length = pieces * nt
    weights = in_ref[layer]
    for k in range(pieces):
        gather[:, k * nt : (k + 1) * nt, :] = chunks[k][...].astype(F32)
    everyone = norm32(gather[...].reshape(nb * length, width))
    mine = jnp.concatenate([everyone[b * length : b * length + span] for b in range(nb)], axis=0)
    base_ref[...] = jnp.concatenate([gather[b, 0:span, :] for b in range(nb)], axis=0)
    query = jnp.dot(mine, weights[:, 0:width], preferred_element_type=F32).astype(BF)
    g_ref[...] = jnp.dot(mine, weights[:, 3 * width :], preferred_element_type=F32).astype(BF)
    keys = jnp.dot(everyone, weights[:, width : 2 * width], preferred_element_type=F32).astype(BF)
    v_ref[...] = jnp.dot(
        everyone, weights[:, 2 * width : 3 * width], preferred_element_type=F32
    ).astype(BF)
    head_of = lax.broadcasted_iota(jnp.int32, (span, width), 1) // (width // heads)
    for b in range(nb):
        q = query[b * span : (b + 1) * span]
        wide = jnp.concatenate(
            [jnp.where(head_of == h, q, jnp.zeros_like(q)) for h in range(heads)], axis=0
        )
        s_ref[b * length : (b + 1) * length] = contract(
            keys[b * length : (b + 1) * length], wide, 1, 1
        )


def attend(heads, span, pieces, s_ref, v_ref, g_ref, base_ref, bias_refs, mask_ref, out_w, table, probs):
    width = v_ref.shape[1]
    length = mask_ref.shape[0]
    nt = length // pieces
    nb = v_ref.shape[0] // length
    scale = (width // heads) ** (-0.5)
    spin = lax.axis_index("gr") ^ lax.axis_index("gc")
    for slot in range(pieces):

        @pl.when(spin == slot)
        def _():
            for k in range(pieces):
                table[k * nt : (k + 1) * nt, :] = bias_refs[slot ^ k][...]

    for b in range(nb):
        s = s_ref[b * length : (b + 1) * length] * scale + table[...] + mask_ref[...]
        e = jnp.exp(s - jnp.max(s, axis=0, keepdims=True))
        probs[b * length : (b + 1) * length] = (
            e * (1.0 / jnp.sum(e, axis=0, keepdims=True))
        ).astype(BF)
    head_of = lax.broadcasted_iota(jnp.int32, (span, width), 1) // (width // heads)
    mixed = []
    for b in range(nb):
        rows = slice(b * length, (b + 1) * length)
        o = contract(probs[rows], v_ref[rows], 0, 0)
        got = o[0:span]
        for h in range(1, heads):
            got = jnp.where(head_of == h, o[h * span : (h + 1) * span], got)
        mixed.append(got)
    mixed = jnp.concatenate(mixed, axis=0)
    gated = (jax.nn.sigmoid(g_ref[...].astype(F32)) * mixed).astype(BF)
    update = jnp.dot(gated, out_w, preferred_element_type=F32)
    return (base_ref[...] + update).astype(BF).astype(F32)


def first_kernel(heads, span, pieces, *refs):
    bias_refs = refs[4 : 4 + pieces]
    (
        mask_ref, out_ref, up_ref, down_ref, weight_ref, chain_ref,
        tile_ref, bias_ref, table, probs, flip,
    ) = refs[4 + pieces :]
    nb = bias_ref.shape[0]
    nt = tile_ref.shape[0]
    first = attend(
        heads, span, pieces, *refs[0:4], bias_refs, mask_ref, out_ref[0], table, probs
    )
    hidden = jnp.dot(norm32(first), up_ref[...], preferred_element_type=F32)
    hidden = jnp.maximum(hidden, 0.0).astype(BF)
    update = jnp.dot(hidden, down_ref[...], preferred_element_type=F32)
    second = (first + update).astype(BF).astype(F32)
    flip[...] = jnp.zeros_like(flip)
    for b in range(nb):
        flip[:, b, :] = second[b * span : b * span + nt]
    turned = flip[...]
    tile_ref[...] = turned[:, 0:nb].astype(BF)
    bias_ref[...] = tile_bias(norm32(turned), weight_ref[1], chain_ref[...], span)[0:nb]


def second_kernel(heads, span, pieces, *refs):
    bias_refs = refs[4 : 4 + pieces]
    mask_ref, out_ref, tile_ref, table, probs, flip = refs[4 + pieces :]
    nt, nb, _ = tile_ref.shape
    last = attend(
        heads, span, pieces, *refs[0:4], bias_refs, mask_ref, out_ref[1], table, probs
    )
    for b in range(nb):
        flip[:, b, :] = last[b * span : b * span + nt]
    tile_ref[...] = flip[...].astype(BF)


VMEM = pl.BlockSpec(memory_space=pltpu.VMEM)
SMEM = pl.BlockSpec(memory_space=pltpu.SMEM)
HBM = pl.BlockSpec(memory_space=pltpu.HBM)
PARAMS = pltpu.CompilerParams(vmem_limit_bytes=24 * 1024 * 1024)


def swap(array, axis, k):
    size = lax.axis_size(axis)
    return lax.ppermute(array, axis, [(i, i ^ k) for i in range(size)])


def scores(layer, heads, span, chunks, weights):
    nb, nt, width = chunks[0].shape
    keys, own, lanes = nb * nt * len(chunks), nb * span, heads * span
    return pl.pallas_call(
        functools.partial(score_kernel, layer, heads, span, len(chunks)),
        out_shape=(
            jax.ShapeDtypeStruct((keys, lanes), F32),
            jax.ShapeDtypeStruct((keys, width), BF),
            jax.ShapeDtypeStruct((own, width), BF),
            jax.ShapeDtypeStruct((own, width), F32),
        ),
        in_specs=[VMEM] * (len(chunks) + 1),
        out_specs=(VMEM,) * 4,
        scratch_shapes=[pltpu.VMEM((nb, len(chunks) * nt, width), F32)],
        compiler_params=PARAMS,
    )(*chunks, weights)


def fast_device(
    span, pair, mask, chain_ids, attn_in, attn_out, bias_weight, chain_bias, trans_up, trans_down
):
    side = lax.axis_size("gc")
    nr, nc, width = pair.shape
    heads = bias_weight.shape[2]
    lanes = heads * span
    cells = [(r, c) for r in range(side) for c in range(side)]
    weight = jnp.transpose(bias_weight, (0, 2, 1))
    plain = (attn_in, attn_out, trans_up, trans_down)

    moved = [swap(pair, "gc", k) for k in range(1, side)]
    piece, chain_two, row_mask, col_mask, own, *plain = pl.pallas_call(
        functools.partial(first_bias_kernel, heads, span, side),
        out_shape=(
            jax.ShapeDtypeStruct((nc, lanes), F32),
            jax.ShapeDtypeStruct((span, lanes), F32),
            jax.ShapeDtypeStruct((side * nc, lanes), F32),
            jax.ShapeDtypeStruct((side * nr, lanes), F32),
            *(jax.ShapeDtypeStruct(a.shape, a.dtype) for a in (pair, *plain)),
        ),
        in_specs=[HBM] * 5 + [VMEM] * 3 + [SMEM],
        out_specs=(VMEM,) * 9,
        scratch_shapes=[
            pltpu.VMEM((nr, span, width), F32),
            pltpu.SemaphoreType.DMA((5,)),
        ],
        compiler_params=PARAMS,
    )(
        *(pltpu.with_memory_space_constraint(a, pltpu.HBM) for a in (pair, *plain)),
        weight, chain_ids[None, :], mask[None, :], chain_bias,
    )
    attn_in, attn_out, trans_up, trans_down = plain
    pieces = []
    for k in range(0, side, 2):
        got = lax.ppermute(
            piece, ("gr", "gc"), [(r * side + c, (c ^ k) * side + r) for r, c in cells]
        )
        pieces += [got, swap(got, "gr", 1)]
    heard = scores(0, heads, span, [own, *moved], attn_in)
    tile, piece = pl.pallas_call(
        functools.partial(first_kernel, heads, span, side),
        out_shape=(
            jax.ShapeDtypeStruct((nc, nr, width), BF),
            jax.ShapeDtypeStruct((nr, lanes), F32),
        ),
        in_specs=[VMEM] * (side + 10),
        out_specs=(VMEM, VMEM),
        scratch_shapes=[
            pltpu.VMEM((side * nc, lanes), F32),
            pltpu.VMEM((nr * side * nc, lanes), BF),
            pltpu.VMEM((nc, span, width), F32),
        ],
        compiler_params=PARAMS,
    )(*heard, *pieces, row_mask, attn_out, trans_up, trans_down, weight, chain_two)

    other = swap(piece, "gr", 1)
    chunks = [tile, swap(tile, "gr", 1)]
    for k in range(2, side, 2):
        far = swap(tile, "gr", k)
        chunks += [far, swap(far, "gr", 1)]
    both = jnp.stack([piece, other])
    pieces = []
    for k in range(0, side, 2):
        got = lax.ppermute(
            both, ("gr", "gc"), [(r * side + c, c * side + (r ^ k)) for r, c in cells]
        )
        pieces += [got[0], got[1]]
    heard = scores(1, heads, span, chunks, attn_in)
    return pl.pallas_call(
        functools.partial(second_kernel, heads, span, side),
        out_shape=jax.ShapeDtypeStruct((nr, nc, width), BF),
        in_specs=[VMEM] * (side + 6),
        out_specs=VMEM,
        scratch_shapes=[
            pltpu.VMEM((side * nr, lanes), F32),
            pltpu.VMEM((nc * side * nr, lanes), BF),
            pltpu.VMEM((nr, nc, width), F32),
        ],
        compiler_params=PARAMS,
    )(*heard, *pieces, col_mask, attn_out)


def solution(mesh):
    shape = dict(mesh.shape)
    in_specs = (P(("jobs", "gr"), "gc", None), P("jobs"), P("jobs"), P(), P(), P(), P(), P(), P())
    out_specs = P(("jobs", "gr"), "gc", None)
    side = shape["gc"]
    square = shape["gr"] == side and side & (side - 1) == 0

    def per_device(*args):
        nr, nc, width = args[0].shape
        heads = args[5].shape[2]
        span = 128 // heads
        fits = nr == nc and nr <= span and (side * nr) % 16 == 0 and width == 128
        if square and fits:
            return fast_device(span, *args)
        return plain_device(*args)

    return jax.shard_map(
        per_device, mesh=mesh, in_specs=in_specs, out_specs=out_specs, check_vma=False
    )
```

```python
import functools

import jax
import jax.numpy as jnp
from jax import lax
from jax.experimental import pallas as pl
from jax.experimental.pallas import tpu as pltpu
from jax.sharding import PartitionSpec as P


BF = jnp.bfloat16
F32 = jnp.float32


def layer_norm(values):
    floats = values.astype(F32)
    center = jnp.mean(floats, axis=-1, keepdims=True)
    spread = jnp.mean((floats - center) ** 2, axis=-1, keepdims=True)
    return ((floats - center) * lax.rsqrt(spread + 1e-05)).astype(BF)


def bias_terms(normed, weight, offset, chain_left, chain_right):
    first, second, width = normed.shape
    heads = weight.shape[1]
    terms = jnp.dot(normed.reshape(-1, width), weight, preferred_element_type=F32)
    same = (chain_left[:, None] == chain_right[None, :]).astype(F32)
    return terms.reshape(first, second, heads) + offset[None, None, :] * same[:, :, None]


def attention(rows, normed, in_w, out_w, bias_full, maskadd):
    count, length, width = rows.shape
    heads = bias_full.shape[0]
    head_width = width // heads
    scale = head_width ** (-0.5)
    proj = jnp.dot(normed.reshape(-1, width), in_w, preferred_element_type=F32)
    proj = proj.astype(BF).reshape(count, length, 4 * width)

    def one_row(piece):
        query = piece[:, 0:width].reshape(length, heads, head_width)
        keys = piece[:, width : 2 * width].reshape(length, heads, head_width)
        vals = piece[:, 2 * width : 3 * width].reshape(length, heads, head_width)
        gate = piece[:, 3 * width :].astype(F32)
        scores = jnp.einsum("jhd,khd->hjk", query, keys, preferred_element_type=F32) * scale
        scores = scores + bias_full + maskadd[None, None, :]
        probs = jax.nn.softmax(scores, axis=-1).astype(BF)
        mixed = jnp.einsum("hjk,khd->jhd", probs, vals, preferred_element_type=F32)
        return (jax.nn.sigmoid(gate) * mixed.reshape(length, width)).astype(BF)

    gated = lax.map(one_row, proj)
    update = jnp.dot(gated.reshape(-1, width), out_w, preferred_element_type=F32)
    return (rows.astype(F32) + update.reshape(rows.shape)).astype(BF)


def transition(rows, trans_up, trans_down):
    width = rows.shape[-1]
    normed = layer_norm(rows).reshape(-1, width)
    hidden = jax.nn.relu(jnp.dot(normed, trans_up, preferred_element_type=F32)).astype(BF)
    update = jnp.dot(hidden, trans_down, preferred_element_type=F32)
    return (rows.astype(F32) + update.reshape(rows.shape)).astype(BF)


def plain_device(
    pair, mask, chain_ids, attn_in, attn_out, bias_weight, chain_bias, trans_up, trans_down
):
    across = lax.axis_size("gc")
    rows = lax.all_to_all(pair, "gc", split_axis=0, concat_axis=1, tiled=True)
    count = rows.shape[0]
    first_row = (lax.axis_index("gr") * across + lax.axis_index("gc")) * count
    maskadd = jnp.where(mask > 0, 0.0, -1000000000.0).astype(F32)
    own_chain = lax.dynamic_slice_in_dim(chain_ids, first_row, count)
    normed = layer_norm(rows)
    start_part = bias_terms(normed, bias_weight[0], chain_bias[0], own_chain, chain_ids)
    start_full = lax.all_gather(
        jnp.transpose(start_part, (2, 0, 1)), ("gr", "gc"), axis=1, tiled=True
    )
    rows = attention(rows, normed, attn_in[0], attn_out[0], start_full, maskadd)
    tile = lax.all_to_all(rows, "gc", split_axis=1, concat_axis=0, tiled=True)
    tile = transition(tile, trans_up, trans_down)
    tile_rows, tile_cols = (tile.shape[0], tile.shape[1])
    chain_rows = lax.dynamic_slice_in_dim(chain_ids, lax.axis_index("gr") * tile_rows, tile_rows)
    chain_cols = lax.dynamic_slice_in_dim(chain_ids, lax.axis_index("gc") * tile_cols, tile_cols)
    end_part = bias_terms(layer_norm(tile), bias_weight[1], chain_bias[1], chain_rows, chain_cols)
    end_part = lax.all_gather(jnp.transpose(end_part, (2, 1, 0)), "gc", axis=1, tiled=True)
    end_full = lax.all_gather(end_part, "gr", axis=2, tiled=True)
    columns = lax.all_to_all(
        jnp.transpose(tile, (1, 0, 2)), "gr", split_axis=0, concat_axis=1, tiled=True
    )
    columns = attention(columns, layer_norm(columns), attn_in[1], attn_out[1], end_full, maskadd)
    returned = lax.all_to_all(columns, "gr", split_axis=1, concat_axis=0, tiled=True)
    return jnp.transpose(returned, (1, 0, 2))


def normal(x):
    center = jnp.mean(x, axis=-1, keepdims=True)
    off = x - center
    spread = jnp.mean(off * off, axis=-1, keepdims=True)
    return off * lax.rsqrt(spread + 1e-05)


def norm32(x):
    return normal(x).astype(BF)


def contract(a, b, da, db):
    return lax.dot_general(a, b, (((da,), (db,)), ((), ())), preferred_element_type=F32)


def every_head(normed, weight, span):
    heads, width = weight.shape
    rep = jnp.concatenate(
        [jnp.broadcast_to(weight[h : h + 1].astype(F32), (span, width)) for h in range(heads)], axis=0
    )
    return contract(normed, rep.astype(BF), 1, 1)


def chain_terms(ids, query_at, key_at, weights, heads, span):
    lanes = heads * span
    reach = ids.shape[1]
    lane = lax.broadcasted_iota(jnp.int32, (reach, lanes), 1) % span
    spot = lax.broadcasted_iota(jnp.int32, (reach, lanes), 0)
    left = contract(ids, (spot == lane + query_at).astype(F32).astype(BF), 1, 0)[0:1]
    row = lax.broadcasted_iota(jnp.int32, (span, reach), 0)
    col = lax.broadcasted_iota(jnp.int32, (span, reach), 1)
    every = jnp.broadcast_to(ids[0:1].astype(F32), (lanes, reach)).astype(BF)
    right = contract((col == row + key_at).astype(F32).astype(BF), every, 1, 1)
    head = lax.broadcasted_iota(jnp.int32, (span, lanes), 1) // span
    term = jnp.zeros((span, lanes), F32)
    for h in range(heads):
        term = jnp.where(head == h, weights[h], term)
    return jnp.where(left == right, term, 0.0)


def key_mask(mask, block, pieces, count, lanes):
    reach = mask.shape[1]
    every = jnp.broadcast_to(mask[0:1].astype(F32), (lanes, reach)).astype(BF)
    shape = (pieces * count, reach)
    row = lax.broadcasted_iota(jnp.int32, shape, 0)
    col = lax.broadcasted_iota(jnp.int32, shape, 1)
    want = jnp.full(shape, -1, jnp.int32)
    for k in range(pieces):
        inside = (row >= k * count) & (row < (k + 1) * count)
        want = jnp.where(inside, row - k * count + (block ^ k) * count, want)
    found = contract((col == want).astype(F32).astype(BF), every, 1, 1)
    return jnp.where(found > 0.0, 0.0, -1000000000.0)


def spread_ids(ref, reach):
    ids = ref[...].astype(F32)
    pad = jnp.zeros((1, reach - ids.shape[1]), F32)
    return jnp.broadcast_to(jnp.concatenate([ids, pad], axis=1), (8, reach)).astype(BF)


def first_bias_kernel(
    heads, span, side, pair_ref, in_ref, out_ref, up_ref, down_ref, weight_ref, ids_ref, mask_ref,
    chain_ref, o_ref, chain_out, row_mask, col_mask, tight, in_out, out_out, up_out, down_out,
    weight_out, own, pad, packed, ids_in, mask_in, chain_in, sems,
):
    nr, nc, width = pair_ref.shape
    rows = pad.shape[1]
    lanes = heads * span
    moves = (
        (ids_ref, ids_in), (mask_ref, mask_in), (chain_ref, chain_in), (weight_ref, weight_out),
        (pair_ref, own), (in_ref, in_out), (out_ref, out_out), (up_ref, up_out),
        (down_ref, down_out),
    )
    copies = [pltpu.make_async_copy(a, b, sems.at[i]) for i, (a, b) in enumerate(moves)]
    for copy in copies:
        copy.start()
    gr, gc = lax.axis_index("gr"), lax.axis_index("gc")
    pad[...] = jnp.zeros_like(pad)
    for copy in copies[0:4]:
        copy.wait()
    ids = spread_ids(ids_in, lanes)
    weights = [[chain_in[a : a + 1, h : h + 1] for h in range(heads)] for a in range(2)]
    here = chain_terms(ids, gr * nr, gc * nc, weights[0], heads, span)
    chain_out[...] = chain_terms(ids, gc * nc, gr * nr, weights[1], heads, span)
    mask = spread_ids(mask_in, lanes)
    row_mask[...] = key_mask(mask, gc, side, nc, lanes)
    col_mask[...] = key_mask(mask, gr, side, nr, lanes)
    copies[4].wait()
    exact = own[...].astype(F32)
    pad[:, 0:nc, :] = exact
    for j in range(nr):
        packed[j * nc : (j + 1) * nc, :] = exact[j]
    tight[...] = packed[...].astype(BF)
    terms = every_head(norm32(pad[...].reshape(nr * rows, width)), weight_out[0], span)
    query_of = lax.broadcasted_iota(jnp.int32, (rows, lanes), 1) % span
    got = here[0:rows]
    for j in range(nr):
        got = got + jnp.where(query_of == j, terms[j * rows : (j + 1) * rows], 0.0)
    o_ref[...] = got[0:nc]
    for copy in copies[5:]:
        copy.wait()


def score_kernel(layer, heads, span, pieces, shape, *refs):
    nb, nt = shape
    in_ref, s_ref, v_ref, g_ref, base_ref, gather = refs[pieces:]
    width = base_ref.shape[1]
    length = pieces * nt
    weights = in_ref[layer]
    for k in range(pieces):
        value = refs[k][...].astype(F32)
        if value.ndim == 3:
            gather[:, k * nt : (k + 1) * nt, :] = value
        else:
            for b in range(nb):
                gather[b, k * nt : (k + 1) * nt, :] = value[b * nt : (b + 1) * nt]
    rows = base_ref.shape[0] // nb
    exact = normal(gather[...].reshape(nb * length, width))
    everyone = exact.astype(BF)
    mine = jnp.concatenate([everyone[b * length : b * length + span] for b in range(nb)], axis=0)
    base_ref[...] = jnp.concatenate([gather[b, 0:rows, :] for b in range(nb)], axis=0)
    query = jnp.dot(mine, weights[:, 0:width], preferred_element_type=F32).astype(BF)
    tight = jnp.concatenate([exact[b * length : b * length + rows] for b in range(nb)], axis=0)
    g_ref[...] = jnp.dot(
        tight.astype(BF), weights[:, 3 * width :], preferred_element_type=F32
    ).astype(BF)
    keys = jnp.dot(everyone, weights[:, width : 2 * width], preferred_element_type=F32).astype(BF)
    v_ref[...] = jnp.dot(
        everyone, weights[:, 2 * width : 3 * width], preferred_element_type=F32
    ).astype(BF)
    head_of = lax.broadcasted_iota(jnp.int32, (span, width), 1) // (width // heads)
    for b in range(nb):
        q = query[b * span : (b + 1) * span]
        wide = jnp.concatenate(
            [jnp.where(head_of == h, q, jnp.zeros_like(q)) for h in range(heads)], axis=0
        )
        s_ref[b * length : (b + 1) * length] = contract(
            keys[b * length : (b + 1) * length], wide, 1, 1
        )


def attend(heads, span, pieces, s_ref, v_ref, g_ref, base_ref, bias_refs, mask_ref, out_w, table, probs):
    width = v_ref.shape[1]
    length = mask_ref.shape[0]
    nt = length // pieces
    nb = v_ref.shape[0] // length
    scale = (width // heads) ** (-0.5)
    spin = lax.axis_index("gr") ^ lax.axis_index("gc")
    for slot in range(pieces):

        @pl.when(spin == slot)
        def _():
            for k in range(pieces):
                table[k * nt : (k + 1) * nt, :] = bias_refs[slot ^ k][...]

    for b in range(nb):
        s = s_ref[b * length : (b + 1) * length] * scale + table[...] + mask_ref[...]
        e = jnp.exp(s - jnp.max(s, axis=0, keepdims=True))
        probs[b * length : (b + 1) * length] = (
            e * (1.0 / jnp.sum(e, axis=0, keepdims=True))
        ).astype(BF)
    rows = base_ref.shape[0] // nb
    head_of = lax.broadcasted_iota(jnp.int32, (rows, width), 1) // (width // heads)
    mixed = []
    for b in range(nb):
        part = slice(b * length, (b + 1) * length)
        o = contract(probs[part], v_ref[part], 0, 0)
        got = o[0:rows]
        for h in range(1, heads):
            got = jnp.where(head_of == h, o[h * span : h * span + rows], got)
        mixed.append(got)
    mixed = jnp.concatenate(mixed, axis=0)
    gated = (jax.nn.sigmoid(g_ref[...].astype(F32)) * mixed).astype(BF)
    update = jnp.dot(gated, out_w, preferred_element_type=F32)
    return (base_ref[...] + update).astype(BF).astype(F32)


def first_kernel(heads, span, pieces, *refs):
    bias_refs = refs[4 : 4 + pieces]
    (
        mask_ref, out_ref, up_ref, down_ref, weight_ref, chain_ref,
        tile_ref, bias_ref, table, probs,
    ) = refs[4 + pieces :]
    nb, lanes = bias_ref.shape
    rows = tile_ref.shape[0] // nb
    first = attend(
        heads, span, pieces, *refs[0:4], bias_refs, mask_ref, out_ref[0], table, probs
    )
    hidden = jnp.dot(norm32(first), up_ref[...], preferred_element_type=F32)
    hidden = jnp.maximum(hidden, 0.0).astype(BF)
    update = jnp.dot(hidden, down_ref[...], preferred_element_type=F32)
    second = (first + update).astype(BF).astype(F32)
    tile_ref[...] = second
    terms = every_head(norm32(second), weight_ref[1], span)
    shape = (rows, lanes)
    pick = lax.broadcasted_iota(jnp.int32, shape, 1) % span == lax.broadcasted_iota(
        jnp.int32, shape, 0
    )
    for b in range(nb):
        line = jnp.where(pick, terms[b * rows : (b + 1) * rows], 0.0)
        bias_ref[b : b + 1, :] = jnp.sum(line, axis=0, keepdims=True) + chain_ref[b : b + 1, :]


def flip_kernel(nb, x_ref, o_ref, flip):
    rows = x_ref.shape[0] // nb
    nt = o_ref.shape[0] // nb
    for b in range(nb):
        flip[pl.ds(b, nt, stride=nb), :] = x_ref[b * rows : b * rows + nt]
    o_ref[...] = flip[...].astype(BF)


def second_kernel(heads, span, pieces, *refs):
    bias_refs = refs[4 : 4 + pieces]
    mask_ref, out_ref, tile_ref, table, probs, flip = refs[4 + pieces :]
    nt, nb, _ = tile_ref.shape
    last = attend(
        heads, span, pieces, *refs[0:4], bias_refs, mask_ref, out_ref[1], table, probs
    )
    rows = last.shape[0] // nb
    for b in range(nb):
        flip[:, b, :] = last[b * rows : b * rows + nt]
    tile_ref[...] = flip[...].astype(BF)


VMEM = pl.BlockSpec(memory_space=pltpu.VMEM)
SMEM = pl.BlockSpec(memory_space=pltpu.SMEM)
HBM = pl.BlockSpec(memory_space=pltpu.HBM)
PARAMS = pltpu.CompilerParams(vmem_limit_bytes=24 * 1024 * 1024)


def up_to_8(count):
    return -(-count // 8) * 8


def swap(array, axis, k):
    size = lax.axis_size(axis)
    return lax.ppermute(array, axis, [(i, i ^ k) for i in range(size)])


def scores(layer, heads, span, shape, chunks, weights):
    nb, nt = shape
    width = weights.shape[1]
    keys, own, lanes = nb * nt * len(chunks), nb * up_to_8(nt), heads * span
    return pl.pallas_call(
        functools.partial(score_kernel, layer, heads, span, len(chunks), shape),
        out_shape=(
            jax.ShapeDtypeStruct((keys, lanes), F32),
            jax.ShapeDtypeStruct((keys, width), BF),
            jax.ShapeDtypeStruct((own, width), BF),
            jax.ShapeDtypeStruct((own, width), F32),
        ),
        in_specs=[VMEM] * (len(chunks) + 1),
        out_specs=(VMEM,) * 4,
        scratch_shapes=[pltpu.VMEM((nb, len(chunks) * nt, width), F32)],
        compiler_params=PARAMS,
    )(*chunks, weights)


def fast_device(
    span, pair, mask, chain_ids, attn_in, attn_out, bias_weight, chain_bias, trans_up, trans_down
):
    side = lax.axis_size("gc")
    nr, nc, width = pair.shape
    heads = bias_weight.shape[2]
    lanes = heads * span
    cells = [(r, c) for r in range(side) for c in range(side)]
    weight = jnp.transpose(bias_weight, (0, 2, 1))
    plain = (attn_in, attn_out, trans_up, trans_down)

    far = swap(pair, "gc", 2)
    sources = (pair, *plain, weight, chain_ids[None, :], mask[None, :], chain_bias)
    copied = (*plain, weight)
    piece, chain_two, row_mask, col_mask, own, *plain, weight = pl.pallas_call(
        functools.partial(first_bias_kernel, heads, span, side),
        out_shape=(
            jax.ShapeDtypeStruct((nc, lanes), F32),
            jax.ShapeDtypeStruct((span, lanes), F32),
            jax.ShapeDtypeStruct((side * nc, lanes), F32),
            jax.ShapeDtypeStruct((side * nr, lanes), F32),
            jax.ShapeDtypeStruct((nr * nc, width), BF),
            *(jax.ShapeDtypeStruct(a.shape, a.dtype) for a in copied),
        ),
        in_specs=[HBM] * len(sources),
        out_specs=(VMEM,) * (5 + len(copied)),
        scratch_shapes=[
            pltpu.VMEM(pair.shape, BF),
            pltpu.VMEM((nr, up_to_8(nc), width), F32),
            pltpu.VMEM((nr * nc, width), F32),
            *(pltpu.VMEM(a.shape, a.dtype) for a in sources[-3:]),
            pltpu.SemaphoreType.DMA((len(sources),)),
        ],
        compiler_params=PARAMS,
    )(*(pltpu.with_memory_space_constraint(a, pltpu.HBM) for a in sources))
    attn_in, attn_out, trans_up, trans_down = plain
    pieces = []
    for k in range(0, side, 2):
        got = lax.ppermute(
            piece, ("gr", "gc"), [(r * side + c, (c ^ k) * side + r) for r, c in cells]
        )
        pieces += [got, swap(got, "gr", 1)]
    last = swap(own, "gc", 3)
    near = swap(own, "gc", 1)
    heard = scores(0, heads, span, (nr, nc), [own, near, far, last], attn_in)
    second, piece = pl.pallas_call(
        functools.partial(first_kernel, heads, span, side),
        out_shape=(
            jax.ShapeDtypeStruct((nr * up_to_8(nc), width), F32),
            jax.ShapeDtypeStruct((nr, lanes), F32),
        ),
        in_specs=[VMEM] * (side + 10),
        out_specs=(VMEM, VMEM),
        scratch_shapes=[
            pltpu.VMEM((side * nc, lanes), F32),
            pltpu.VMEM((nr * side * nc, lanes), BF),
        ],
        compiler_params=PARAMS,
    )(*heard, *pieces, row_mask, attn_out, trans_up, trans_down, weight, chain_two)
    tile = pl.pallas_call(
        functools.partial(flip_kernel, nr),
        out_shape=jax.ShapeDtypeStruct((nc * nr, width), BF),
        in_specs=[VMEM],
        out_specs=VMEM,
        scratch_shapes=[pltpu.VMEM((nc * nr, width), F32)],
        compiler_params=PARAMS,
    )(second)

    other = swap(piece, "gr", 1)
    chunks = [tile, swap(tile, "gr", 1)]
    for k in range(2, side, 2):
        far = swap(tile, "gr", k)
        chunks += [far, swap(far, "gr", 1)]
    both = jnp.stack([piece, other])
    pieces = []
    for k in range(0, side, 2):
        got = lax.ppermute(
            both, ("gr", "gc"), [(r * side + c, c * side + (r ^ k)) for r, c in cells]
        )
        pieces += [got[0], got[1]]
    heard = scores(1, heads, span, (nc, nr), chunks, attn_in)
    return pl.pallas_call(
        functools.partial(second_kernel, heads, span, side),
        out_shape=jax.ShapeDtypeStruct((nr, nc, width), BF),
        in_specs=[VMEM] * (side + 6),
        out_specs=VMEM,
        scratch_shapes=[
            pltpu.VMEM((side * nr, lanes), F32),
            pltpu.VMEM((nc * side * nr, lanes), BF),
            pltpu.VMEM((nr, nc, width), F32),
        ],
        compiler_params=PARAMS,
    )(*heard, *pieces, col_mask, attn_out)


def solution(mesh):
    shape = dict(mesh.shape)
    in_specs = (P(("jobs", "gr"), "gc", None), P("jobs"), P("jobs"), P(), P(), P(), P(), P(), P())
    out_specs = P(("jobs", "gr"), "gc", None)
    side = shape["gc"]
    square = shape["gr"] == side and side == 4

    def per_device(*args):
        nr, nc, width = args[0].shape
        heads = args[5].shape[2]
        span = 128 // heads
        fits = nr == nc and nr <= span and (side * nr) % 16 == 0 and width == 128
        if square and fits:
            return fast_device(span, *args)
        return plain_device(*args)

    return jax.shard_map(
        per_device, mesh=mesh, in_specs=in_specs, out_specs=out_specs, check_vma=False
    )
```

```python
import functools

import jax
import jax.numpy as jnp
from jax import lax
from jax.experimental import pallas as pl
from jax.experimental.pallas import tpu as pltpu
from jax.sharding import PartitionSpec as P


BF = jnp.bfloat16
GROUPS = 1
LOG2E = 1.4426950408889634
F32 = jnp.float32


def layer_norm(values):
    floats = values.astype(F32)
    center = jnp.mean(floats, axis=-1, keepdims=True)
    spread = jnp.mean((floats - center) ** 2, axis=-1, keepdims=True)
    return ((floats - center) * lax.rsqrt(spread + 1e-05)).astype(BF)


def bias_terms(normed, weight, offset, chain_left, chain_right):
    first, second, width = normed.shape
    heads = weight.shape[1]
    terms = jnp.dot(normed.reshape(-1, width), weight, preferred_element_type=F32)
    same = (chain_left[:, None] == chain_right[None, :]).astype(F32)
    return terms.reshape(first, second, heads) + offset[None, None, :] * same[:, :, None]


def attention(rows, normed, in_w, out_w, bias_full, maskadd):
    count, length, width = rows.shape
    heads = bias_full.shape[0]
    head_width = width // heads
    scale = head_width ** (-0.5)
    proj = jnp.dot(normed.reshape(-1, width), in_w, preferred_element_type=F32)
    proj = proj.astype(BF).reshape(count, length, 4 * width)

    def one_row(piece):
        query = piece[:, 0:width].reshape(length, heads, head_width)
        keys = piece[:, width : 2 * width].reshape(length, heads, head_width)
        vals = piece[:, 2 * width : 3 * width].reshape(length, heads, head_width)
        gate = piece[:, 3 * width :].astype(F32)
        scores = jnp.einsum("jhd,khd->hjk", query, keys, preferred_element_type=F32) * scale
        scores = scores + bias_full + maskadd[None, None, :]
        probs = jax.nn.softmax(scores, axis=-1).astype(BF)
        mixed = jnp.einsum("hjk,khd->jhd", probs, vals, preferred_element_type=F32)
        return (jax.nn.sigmoid(gate) * mixed.reshape(length, width)).astype(BF)

    gated = lax.map(one_row, proj)
    update = jnp.dot(gated.reshape(-1, width), out_w, preferred_element_type=F32)
    return (rows.astype(F32) + update.reshape(rows.shape)).astype(BF)


def transition(rows, trans_up, trans_down):
    width = rows.shape[-1]
    normed = layer_norm(rows).reshape(-1, width)
    hidden = jax.nn.relu(jnp.dot(normed, trans_up, preferred_element_type=F32)).astype(BF)
    update = jnp.dot(hidden, trans_down, preferred_element_type=F32)
    return (rows.astype(F32) + update.reshape(rows.shape)).astype(BF)


def plain_device(
    pair, mask, chain_ids, attn_in, attn_out, bias_weight, chain_bias, trans_up, trans_down
):
    across = lax.axis_size("gc")
    rows = lax.all_to_all(pair, "gc", split_axis=0, concat_axis=1, tiled=True)
    count = rows.shape[0]
    first_row = (lax.axis_index("gr") * across + lax.axis_index("gc")) * count
    maskadd = jnp.where(mask > 0, 0.0, -1000000000.0).astype(F32)
    own_chain = lax.dynamic_slice_in_dim(chain_ids, first_row, count)
    normed = layer_norm(rows)
    start_part = bias_terms(normed, bias_weight[0], chain_bias[0], own_chain, chain_ids)
    start_full = lax.all_gather(
        jnp.transpose(start_part, (2, 0, 1)), ("gr", "gc"), axis=1, tiled=True
    )
    rows = attention(rows, normed, attn_in[0], attn_out[0], start_full, maskadd)
    tile = lax.all_to_all(rows, "gc", split_axis=1, concat_axis=0, tiled=True)
    tile = transition(tile, trans_up, trans_down)
    tile_rows, tile_cols = (tile.shape[0], tile.shape[1])
    chain_rows = lax.dynamic_slice_in_dim(chain_ids, lax.axis_index("gr") * tile_rows, tile_rows)
    chain_cols = lax.dynamic_slice_in_dim(chain_ids, lax.axis_index("gc") * tile_cols, tile_cols)
    end_part = bias_terms(layer_norm(tile), bias_weight[1], chain_bias[1], chain_rows, chain_cols)
    end_part = lax.all_gather(jnp.transpose(end_part, (2, 1, 0)), "gc", axis=1, tiled=True)
    end_full = lax.all_gather(end_part, "gr", axis=2, tiled=True)
    columns = lax.all_to_all(
        jnp.transpose(tile, (1, 0, 2)), "gr", split_axis=0, concat_axis=1, tiled=True
    )
    columns = attention(columns, layer_norm(columns), attn_in[1], attn_out[1], end_full, maskadd)
    returned = lax.all_to_all(columns, "gr", split_axis=1, concat_axis=0, tiled=True)
    return jnp.transpose(returned, (1, 0, 2))


def normal(x):
    center = jnp.mean(x, axis=-1, keepdims=True)
    off = x - center
    spread = jnp.mean(off * off, axis=-1, keepdims=True)
    return off * lax.rsqrt(spread + 1e-05)


def norm32(x):
    return normal(x).astype(BF)


def contract(a, b, da, db):
    return lax.dot_general(a, b, (((da,), (db,)), ((), ())), preferred_element_type=F32)


def every_head(normed, weight, span):
    heads, width = weight.shape
    rep = jnp.concatenate(
        [jnp.broadcast_to(weight[h : h + 1].astype(F32), (span, width)) for h in range(heads)], axis=0
    )
    return contract(normed, rep.astype(BF), 1, 1)


def select_terms(terms, chain, rows, count, span):
    query_of = lax.broadcasted_iota(jnp.int32, (rows, terms.shape[1]), 1) % span
    got = jnp.zeros((rows, terms.shape[1]), F32)
    for j in range(count):
        got = jnp.where(query_of == j, terms[j * rows : (j + 1) * rows], got)
    return got + chain


def chain_terms(ids, query_at, key_at, weights, heads, span):
    lanes = heads * span
    reach = ids.shape[1]
    lane = lax.broadcasted_iota(jnp.int32, (reach, lanes), 1) % span
    spot = lax.broadcasted_iota(jnp.int32, (reach, lanes), 0)
    left = contract(ids, (spot == lane + query_at).astype(F32).astype(BF), 1, 0)[0:1]
    row = lax.broadcasted_iota(jnp.int32, (span, reach), 0)
    col = lax.broadcasted_iota(jnp.int32, (span, reach), 1)
    every = jnp.broadcast_to(ids[0:1].astype(F32), (lanes, reach)).astype(BF)
    right = contract((col == row + key_at).astype(F32).astype(BF), every, 1, 1)
    head = lax.broadcasted_iota(jnp.int32, (span, lanes), 1) // span
    term = jnp.zeros((span, lanes), F32)
    for h in range(heads):
        term = jnp.where(head == h, weights[h], term)
    return jnp.where(left == right, term, 0.0)


def key_mask(mask, block, pieces, count, lanes):
    reach = mask.shape[1]
    every = jnp.broadcast_to(mask[0:1].astype(F32), (lanes, reach)).astype(BF)
    shape = (pieces * count, reach)
    row = lax.broadcasted_iota(jnp.int32, shape, 0)
    col = lax.broadcasted_iota(jnp.int32, shape, 1)
    want = jnp.full(shape, -1, jnp.int32)
    for k in range(pieces):
        inside = (row >= k * count) & (row < (k + 1) * count)
        want = jnp.where(inside, row - k * count + (block ^ k) * count, want)
    found = contract((col == want).astype(F32).astype(BF), every, 1, 1)
    return jnp.where(found > 0.0, 0.0, -1000000000.0)


def spread_ids(ref, reach):
    ids = ref[...].astype(F32)
    pad = jnp.zeros((1, reach - ids.shape[1]), F32)
    return jnp.broadcast_to(jnp.concatenate([ids, pad], axis=1), (8, reach)).astype(BF)


def first_bias_kernel(
    heads, span, side, pair_ref, in_ref, out_ref, up_ref, down_ref, weight_ref, ids_ref, mask_ref,
    chain_ref, o_ref, chain_out, row_mask, col_mask, tight, in_out, out_out, up_out, down_out,
    weight_out, own, pad, packed, ids_in, mask_in, chain_in, sems,
):
    nr, nc, width = pair_ref.shape
    rows = pad.shape[1]
    lanes = heads * span
    moves = (
        (ids_ref, ids_in), (mask_ref, mask_in), (chain_ref, chain_in), (weight_ref, weight_out),
        (pair_ref, own), (in_ref, in_out), (out_ref, out_out), (up_ref, up_out),
        (down_ref, down_out),
    )
    copies = [pltpu.make_async_copy(a, b, sems.at[i]) for i, (a, b) in enumerate(moves)]
    for copy in copies:
        copy.start()
    gr, gc = lax.axis_index("gr"), lax.axis_index("gc")
    pad[...] = jnp.zeros_like(pad)
    for copy in copies[0:4]:
        copy.wait()
    ids = spread_ids(ids_in, lanes)
    weights = [[chain_in[a : a + 1, h : h + 1] for h in range(heads)] for a in range(2)]
    here = chain_terms(ids, gr * nr, gc * nc, weights[0], heads, span)
    chain_out[...] = chain_terms(ids, gc * nc, gr * nr, weights[1], heads, span)[
        0 : chain_out.shape[0]
    ]
    mask = spread_ids(mask_in, lanes)
    row_mask[...] = key_mask(mask, gc, side, nc, lanes)
    col_mask[...] = key_mask(mask, gr, side, nr, lanes)
    copies[4].wait()
    exact = own[...].astype(F32)
    pad[:, 0:nc, :] = exact
    for j in range(nr):
        packed[j * nc : (j + 1) * nc, :] = exact[j]
    tight[...] = packed[...].astype(BF)
    terms = every_head(norm32(pad[...].reshape(nr * rows, width)), weight_out[0], span)
    o_ref[...] = select_terms(terms, here[0:rows], rows, nr, span)[0:nc]
    for copy in copies[5:]:
        copy.wait()


def score_kernel(layer, heads, span, pieces, shape, *refs):
    nb, nt = shape
    in_ref, s_ref, v_ref, g_ref, base_ref, gather = refs[pieces:]
    width = base_ref.shape[1]
    length = pieces * nt
    weights = in_ref[layer]
    for k in range(pieces):
        value = refs[k][...].astype(F32)
        if value.ndim == 3:
            gather[:, k * nt : (k + 1) * nt, :] = value
        else:
            for b in range(nb):
                gather[b, k * nt : (k + 1) * nt, :] = value[b * nt : (b + 1) * nt]
    rows = base_ref.shape[0] // nb
    exact = normal(gather[...].reshape(nb * length, width))
    everyone = exact.astype(BF)
    mine = jnp.concatenate([everyone[b * length : b * length + span] for b in range(nb)], axis=0)
    base_ref[...] = jnp.concatenate([gather[b, 0:rows, :] for b in range(nb)], axis=0)
    query = jnp.dot(mine, weights[:, 0:width], preferred_element_type=F32).astype(BF)
    tight = jnp.concatenate([exact[b * length : b * length + rows] for b in range(nb)], axis=0)
    g_ref[...] = jnp.dot(
        tight.astype(BF), weights[:, 3 * width :], preferred_element_type=F32
    ).astype(BF)
    keys = jnp.dot(everyone, weights[:, width : 2 * width], preferred_element_type=F32).astype(BF)
    v_ref[...] = jnp.dot(
        everyone, weights[:, 2 * width : 3 * width], preferred_element_type=F32
    ).astype(BF)
    head_of = lax.broadcasted_iota(jnp.int32, (span, width), 1) // (width // heads)
    scale = LOG2E * (width // heads) ** (-0.5)
    for b in range(nb):
        q = query[b * span : (b + 1) * span]
        wide = jnp.concatenate(
            [jnp.where(head_of == h, q, jnp.zeros_like(q)) for h in range(heads)], axis=0
        )
        s_ref[b * length : (b + 1) * length] = scale * contract(
            keys[b * length : (b + 1) * length], wide, 1, 1
        )


def attend(heads, span, pieces, s_ref, v_ref, g_ref, base_ref, bias_refs, mask_ref, out_w, table, probs):
    width = v_ref.shape[1]
    length = mask_ref.shape[0]
    nt = length // pieces
    nb = v_ref.shape[0] // length
    spin = lax.axis_index("gr") ^ lax.axis_index("gc")
    for slot in range(pieces):

        @pl.when(spin == slot)
        def _():
            for k in range(pieces):
                table[k * nt : (k + 1) * nt, :] = bias_refs[slot ^ k][...]

    shift = LOG2E * (table[...] + mask_ref[...])
    for b in range(nb):
        s = s_ref[b * length : (b + 1) * length] + shift
        e = jnp.exp2(s - jnp.max(s, axis=0, keepdims=True))
        probs[b * length : (b + 1) * length] = (
            e * (1.0 / jnp.sum(e, axis=0, keepdims=True))
        ).astype(BF)
    rows = base_ref.shape[0] // nb
    head_of = lax.broadcasted_iota(jnp.int32, (rows, width), 1) // (width // heads)
    done = []
    for group in range(GROUPS):
        mine = range(group * nb // GROUPS, (group + 1) * nb // GROUPS)
        mixed = []
        for b in mine:
            part = slice(b * length, (b + 1) * length)
            o = contract(probs[part], v_ref[part], 0, 0)
            got = o[0:rows]
            for h in range(1, heads):
                got = jnp.where(head_of == h, o[h * span : h * span + rows], got)
            mixed.append(got)
        part = slice(mine[0] * rows, (mine[-1] + 1) * rows)
        gate = jax.nn.sigmoid(g_ref[part].astype(F32))
        gated = (gate * jnp.concatenate(mixed, axis=0)).astype(BF)
        update = jnp.dot(gated, out_w, preferred_element_type=F32)
        done.append((base_ref[part] + update).astype(BF).astype(F32))
    return done


def first_kernel(heads, span, pieces, *refs):
    bias_refs = refs[4 : 4 + pieces]
    (
        mask_ref, out_ref, up_ref, down_ref, weight_ref, chain_ref,
        tile_ref, bias_ref, table, probs, turned,
    ) = refs[4 + pieces :]
    nb, _ = bias_ref.shape
    rows = tile_ref.shape[0] // nb
    done = attend(
        heads, span, pieces, *refs[0:4], bias_refs, mask_ref, out_ref[0], table, probs
    )
    parts = []
    for first in done:
        hidden = jnp.dot(norm32(first), up_ref[...], preferred_element_type=F32)
        hidden = jnp.maximum(hidden, 0.0).astype(BF)
        update = jnp.dot(hidden, down_ref[...], preferred_element_type=F32)
        parts.append((first + update).astype(BF).astype(F32))
    second = jnp.concatenate(parts, axis=0)
    tile_ref[...] = second
    nt = turned.shape[0] // rows
    turned[...] = jnp.zeros_like(turned)
    for b in range(nb):
        turned[pl.ds(b, nt, stride=rows), :] = second[b * rows : b * rows + nt]
    bias_ref[...] = select_terms(
        every_head(norm32(turned[...]), weight_ref[1], span), chain_ref[...], rows, nt, span
    )[0:nb]


def flip_kernel(nb, x_ref, o_ref, flip):
    rows = x_ref.shape[0] // nb
    nt = o_ref.shape[0] // nb
    for b in range(nb):
        flip[pl.ds(b, nt, stride=nb), :] = x_ref[b * rows : b * rows + nt]
    o_ref[...] = flip[...].astype(BF)


def second_kernel(heads, span, pieces, *refs):
    bias_refs = refs[4 : 4 + pieces]
    mask_ref, out_ref, tile_ref, table, probs, flip = refs[4 + pieces :]
    nt, nb, _ = tile_ref.shape
    done = attend(
        heads, span, pieces, *refs[0:4], bias_refs, mask_ref, out_ref[1], table, probs
    )
    last = jnp.concatenate(done, axis=0)
    rows = last.shape[0] // nb
    room = flip.shape[0] // nt
    for b in range(nb):
        flip[pl.ds(b, nt, stride=room), :] = last[b * rows : b * rows + nt]
    tile_ref[...] = flip[...].reshape(nt, room, -1)[:, 0:nb].astype(BF)


VMEM = pl.BlockSpec(memory_space=pltpu.VMEM)
SMEM = pl.BlockSpec(memory_space=pltpu.SMEM)
HBM = pl.BlockSpec(memory_space=pltpu.HBM)
PARAMS = pltpu.CompilerParams(vmem_limit_bytes=24 * 1024 * 1024)


def up_to_8(count):
    return -(-count // 8) * 8


def swap(array, axis, k):
    size = lax.axis_size(axis)
    return lax.ppermute(array, axis, [(i, i ^ k) for i in range(size)])


def scores(layer, heads, span, shape, chunks, weights):
    nb, nt = shape
    width = weights.shape[1]
    keys, own, lanes = nb * nt * len(chunks), nb * up_to_8(nt), heads * span
    return pl.pallas_call(
        functools.partial(score_kernel, layer, heads, span, len(chunks), shape),
        out_shape=(
            jax.ShapeDtypeStruct((keys, lanes), F32),
            jax.ShapeDtypeStruct((keys, width), BF),
            jax.ShapeDtypeStruct((own, width), BF),
            jax.ShapeDtypeStruct((own, width), F32),
        ),
        in_specs=[VMEM] * (len(chunks) + 1),
        out_specs=(VMEM,) * 4,
        scratch_shapes=[pltpu.VMEM((nb, len(chunks) * nt, width), F32)],
        compiler_params=PARAMS,
    )(*chunks, weights)


def fast_device(
    span, pair, mask, chain_ids, attn_in, attn_out, bias_weight, chain_bias, trans_up, trans_down
):
    side = lax.axis_size("gc")
    nr, nc, width = pair.shape
    heads = bias_weight.shape[2]
    lanes = heads * span
    cells = [(r, c) for r in range(side) for c in range(side)]
    weight = jnp.transpose(bias_weight, (0, 2, 1))
    plain = (attn_in, attn_out, trans_up, trans_down)

    far = swap(pair, "gc", 2)
    sources = (pair, *plain, weight, chain_ids[None, :], mask[None, :], chain_bias)
    copied = (*plain, weight)
    piece, chain_two, row_mask, col_mask, own, *plain, weight = pl.pallas_call(
        functools.partial(first_bias_kernel, heads, span, side),
        out_shape=(
            jax.ShapeDtypeStruct((nc, lanes), F32),
            jax.ShapeDtypeStruct((up_to_8(nr), lanes), F32),
            jax.ShapeDtypeStruct((side * nc, lanes), F32),
            jax.ShapeDtypeStruct((side * nr, lanes), F32),
            jax.ShapeDtypeStruct((nr * nc, width), BF),
            *(jax.ShapeDtypeStruct(a.shape, a.dtype) for a in copied),
        ),
        in_specs=[HBM] * len(sources),
        out_specs=(VMEM,) * (5 + len(copied)),
        scratch_shapes=[
            pltpu.VMEM(pair.shape, BF),
            pltpu.VMEM((nr, up_to_8(nc), width), F32),
            pltpu.VMEM((nr * nc, width), F32),
            *(pltpu.VMEM(a.shape, a.dtype) for a in sources[-3:]),
            pltpu.SemaphoreType.DMA((len(sources),)),
        ],
        compiler_params=PARAMS,
    )(*(pltpu.with_memory_space_constraint(a, pltpu.HBM) for a in sources))
    attn_in, attn_out, trans_up, trans_down = plain
    pieces = []
    for k in range(0, side, 2):
        got = lax.ppermute(
            piece, ("gr", "gc"), [(r * side + c, (c ^ k) * side + r) for r, c in cells]
        )
        pieces += [got, swap(got, "gr", 1)]
    last = swap(own, "gc", 3)
    near = swap(own, "gc", 1)
    heard = scores(0, heads, span, (nr, nc), [own, near, far, last], attn_in)
    second, piece = pl.pallas_call(
        functools.partial(first_kernel, heads, span, side),
        out_shape=(
            jax.ShapeDtypeStruct((nr * up_to_8(nc), width), F32),
            jax.ShapeDtypeStruct((nr, lanes), F32),
        ),
        in_specs=[VMEM] * (side + 10),
        out_specs=(VMEM, VMEM),
        scratch_shapes=[
            pltpu.VMEM((side * nc, lanes), F32),
            pltpu.VMEM((nr * side * nc, lanes), BF),
            pltpu.VMEM((nc * up_to_8(nr), width), F32),
        ],
        compiler_params=PARAMS,
    )(*heard, *pieces, row_mask, attn_out, trans_up, trans_down, weight, chain_two)
    tile = pl.pallas_call(
        functools.partial(flip_kernel, nr),
        out_shape=jax.ShapeDtypeStruct((nc * nr, width), BF),
        in_specs=[VMEM],
        out_specs=VMEM,
        scratch_shapes=[pltpu.VMEM((nc * nr, width), F32)],
        compiler_params=PARAMS,
    )(second)

    other = swap(piece, "gr", 1)
    chunks = [tile, swap(tile, "gr", 1)]
    for k in range(2, side, 2):
        far = swap(tile, "gr", k)
        chunks += [far, swap(far, "gr", 1)]
    both = jnp.stack([piece, other])
    pieces = []
    for k in range(0, side, 2):
        got = lax.ppermute(
            both, ("gr", "gc"), [(r * side + c, c * side + (r ^ k)) for r, c in cells]
        )
        pieces += [got[0], got[1]]
    heard = scores(1, heads, span, (nc, nr), chunks, attn_in)
    return pl.pallas_call(
        functools.partial(second_kernel, heads, span, side),
        out_shape=jax.ShapeDtypeStruct((nr, nc, width), BF),
        in_specs=[VMEM] * (side + 6),
        out_specs=VMEM,
        scratch_shapes=[
            pltpu.VMEM((side * nr, lanes), F32),
            pltpu.VMEM((nc * side * nr, lanes), BF),
            pltpu.VMEM((nr * up_to_8(nc), width), F32),
        ],
        compiler_params=PARAMS,
    )(*heard, *pieces, col_mask, attn_out)


def solution(mesh):
    shape = dict(mesh.shape)
    in_specs = (P(("jobs", "gr"), "gc", None), P("jobs"), P("jobs"), P(), P(), P(), P(), P(), P())
    out_specs = P(("jobs", "gr"), "gc", None)
    side = shape["gc"]
    square = shape["gr"] == side and side == 4

    def per_device(*args):
        nr, nc, width = args[0].shape
        heads = args[5].shape[2]
        span = 128 // heads
        fits = nr == nc and nr <= span and (side * nr) % 16 == 0 and width == 128
        if square and fits:
            return fast_device(span, *args)
        return plain_device(*args)

    return jax.shard_map(
        per_device, mesh=mesh, in_specs=in_specs, out_specs=out_specs, check_vma=False
    )
```

```python
import functools

import jax
import jax.numpy as jnp
from jax import lax
from jax.experimental import pallas as pl
from jax.experimental.pallas import tpu as pltpu
from jax.sharding import PartitionSpec as P


BF = jnp.bfloat16
GROUPS = 1
LOG2E = 1.4426950408889634
F32 = jnp.float32


def layer_norm(values):
    floats = values.astype(F32)
    center = jnp.mean(floats, axis=-1, keepdims=True)
    spread = jnp.mean((floats - center) ** 2, axis=-1, keepdims=True)
    return ((floats - center) * lax.rsqrt(spread + 1e-05)).astype(BF)


def bias_terms(normed, weight, offset, chain_left, chain_right):
    first, second, width = normed.shape
    heads = weight.shape[1]
    terms = jnp.dot(normed.reshape(-1, width), weight, preferred_element_type=F32)
    same = (chain_left[:, None] == chain_right[None, :]).astype(F32)
    return terms.reshape(first, second, heads) + offset[None, None, :] * same[:, :, None]


def attention(rows, normed, in_w, out_w, bias_full, maskadd):
    count, length, width = rows.shape
    heads = bias_full.shape[0]
    head_width = width // heads
    scale = head_width ** (-0.5)
    proj = jnp.dot(normed.reshape(-1, width), in_w, preferred_element_type=F32)
    proj = proj.astype(BF).reshape(count, length, 4 * width)

    def one_row(piece):
        query = piece[:, 0:width].reshape(length, heads, head_width)
        keys = piece[:, width : 2 * width].reshape(length, heads, head_width)
        vals = piece[:, 2 * width : 3 * width].reshape(length, heads, head_width)
        gate = piece[:, 3 * width :].astype(F32)
        scores = jnp.einsum("jhd,khd->hjk", query, keys, preferred_element_type=F32) * scale
        scores = scores + bias_full + maskadd[None, None, :]
        probs = jax.nn.softmax(scores, axis=-1).astype(BF)
        mixed = jnp.einsum("hjk,khd->jhd", probs, vals, preferred_element_type=F32)
        return (jax.nn.sigmoid(gate) * mixed.reshape(length, width)).astype(BF)

    gated = lax.map(one_row, proj)
    update = jnp.dot(gated.reshape(-1, width), out_w, preferred_element_type=F32)
    return (rows.astype(F32) + update.reshape(rows.shape)).astype(BF)


def transition(rows, trans_up, trans_down):
    width = rows.shape[-1]
    normed = layer_norm(rows).reshape(-1, width)
    hidden = jax.nn.relu(jnp.dot(normed, trans_up, preferred_element_type=F32)).astype(BF)
    update = jnp.dot(hidden, trans_down, preferred_element_type=F32)
    return (rows.astype(F32) + update.reshape(rows.shape)).astype(BF)


def plain_device(
    pair, mask, chain_ids, attn_in, attn_out, bias_weight, chain_bias, trans_up, trans_down
):
    across = lax.axis_size("gc")
    rows = lax.all_to_all(pair, "gc", split_axis=0, concat_axis=1, tiled=True)
    count = rows.shape[0]
    first_row = (lax.axis_index("gr") * across + lax.axis_index("gc")) * count
    maskadd = jnp.where(mask > 0, 0.0, -1000000000.0).astype(F32)
    own_chain = lax.dynamic_slice_in_dim(chain_ids, first_row, count)
    normed = layer_norm(rows)
    start_part = bias_terms(normed, bias_weight[0], chain_bias[0], own_chain, chain_ids)
    start_full = lax.all_gather(
        jnp.transpose(start_part, (2, 0, 1)), ("gr", "gc"), axis=1, tiled=True
    )
    rows = attention(rows, normed, attn_in[0], attn_out[0], start_full, maskadd)
    tile = lax.all_to_all(rows, "gc", split_axis=1, concat_axis=0, tiled=True)
    tile = transition(tile, trans_up, trans_down)
    tile_rows, tile_cols = (tile.shape[0], tile.shape[1])
    chain_rows = lax.dynamic_slice_in_dim(chain_ids, lax.axis_index("gr") * tile_rows, tile_rows)
    chain_cols = lax.dynamic_slice_in_dim(chain_ids, lax.axis_index("gc") * tile_cols, tile_cols)
    end_part = bias_terms(layer_norm(tile), bias_weight[1], chain_bias[1], chain_rows, chain_cols)
    end_part = lax.all_gather(jnp.transpose(end_part, (2, 1, 0)), "gc", axis=1, tiled=True)
    end_full = lax.all_gather(end_part, "gr", axis=2, tiled=True)
    columns = lax.all_to_all(
        jnp.transpose(tile, (1, 0, 2)), "gr", split_axis=0, concat_axis=1, tiled=True
    )
    columns = attention(columns, layer_norm(columns), attn_in[1], attn_out[1], end_full, maskadd)
    returned = lax.all_to_all(columns, "gr", split_axis=1, concat_axis=0, tiled=True)
    return jnp.transpose(returned, (1, 0, 2))


def normal(x):
    center = jnp.mean(x, axis=-1, keepdims=True)
    off = x - center
    spread = jnp.mean(off * off, axis=-1, keepdims=True)
    return off * lax.rsqrt(spread + 1e-05)


def norm32(x):
    return normal(x).astype(BF)


def contract(a, b, da, db):
    return lax.dot_general(a, b, (((da,), (db,)), ((), ())), preferred_element_type=F32)


def every_head(normed, weight, span):
    heads, width = weight.shape
    rep = jnp.concatenate(
        [jnp.broadcast_to(weight[h : h + 1].astype(F32), (span, width)) for h in range(heads)], axis=0
    )
    return contract(normed, rep.astype(BF), 1, 1)


def select_terms(terms, chain, rows, count, span):
    query_of = lax.broadcasted_iota(jnp.int32, (rows, terms.shape[1]), 1) % span
    got = jnp.zeros((rows, terms.shape[1]), F32)
    for j in range(count):
        got = jnp.where(query_of == j, terms[j * rows : (j + 1) * rows], got)
    return got + chain


def chain_terms(ids, query_at, key_at, weights, heads, span):
    lanes = heads * span
    reach = ids.shape[1]
    lane = lax.broadcasted_iota(jnp.int32, (reach, lanes), 1) % span
    spot = lax.broadcasted_iota(jnp.int32, (reach, lanes), 0)
    left = contract(ids, (spot == lane + query_at).astype(F32).astype(BF), 1, 0)[0:1]
    row = lax.broadcasted_iota(jnp.int32, (span, reach), 0)
    col = lax.broadcasted_iota(jnp.int32, (span, reach), 1)
    every = jnp.broadcast_to(ids[0:1].astype(F32), (lanes, reach)).astype(BF)
    right = contract((col == row + key_at).astype(F32).astype(BF), every, 1, 1)
    head = lax.broadcasted_iota(jnp.int32, (span, lanes), 1) // span
    term = jnp.zeros((span, lanes), F32)
    for h in range(heads):
        term = jnp.where(head == h, weights[h], term)
    return jnp.where(left == right, term, 0.0)


def key_mask(mask, block, pieces, count, lanes):
    reach = mask.shape[1]
    every = jnp.broadcast_to(mask[0:1].astype(F32), (lanes, reach)).astype(BF)
    shape = (pieces * count, reach)
    row = lax.broadcasted_iota(jnp.int32, shape, 0)
    col = lax.broadcasted_iota(jnp.int32, shape, 1)
    want = jnp.full(shape, -1, jnp.int32)
    for k in range(pieces):
        inside = (row >= k * count) & (row < (k + 1) * count)
        want = jnp.where(inside, row - k * count + (block ^ k) * count, want)
    found = contract((col == want).astype(F32).astype(BF), every, 1, 1)
    return jnp.where(found > 0.0, 0.0, -1000000000.0)


def spread_ids(ref, reach):
    ids = ref[...].astype(F32)
    pad = jnp.zeros((1, reach - ids.shape[1]), F32)
    return jnp.broadcast_to(jnp.concatenate([ids, pad], axis=1), (8, reach)).astype(BF)


def copies_of(moves, sems):
    copies = [pltpu.make_async_copy(a, b, sems.at[i]) for i, (a, b) in enumerate(moves)]
    for copy in copies:
        copy.start()
    return copies


def chain_weights(ref, layer, heads):
    return [ref[layer : layer + 1, h : h + 1] for h in range(heads)]


def first_bias_kernel(
    heads, span, pair_ref, weight_ref, ids_ref, chain_ref, o_ref, tight,
    own, pad, packed, weight_in, ids_in, chain_in, sems,
):
    nr, nc, width = pair_ref.shape
    rows = pad.shape[1]
    lanes = heads * span
    copies = copies_of(
        ((pair_ref, own), (weight_ref, weight_in), (ids_ref, ids_in), (chain_ref, chain_in)), sems
    )
    gr, gc = lax.axis_index("gr"), lax.axis_index("gc")
    pad[...] = jnp.zeros_like(pad)
    for copy in copies[1:]:
        copy.wait()
    ids = spread_ids(ids_in, lanes)
    here = chain_terms(ids, gr * nr, gc * nc, chain_weights(chain_in, 0, heads), heads, span)
    copies[0].wait()
    exact = own[...].astype(F32)
    pad[:, 0:nc, :] = exact
    for j in range(nr):
        packed[j * nc : (j + 1) * nc, :] = exact[j]
    tight[...] = packed[...].astype(BF)
    terms = every_head(norm32(pad[...].reshape(nr * rows, width)), weight_in[0], span)
    o_ref[...] = select_terms(terms, here[0:rows], rows, nr, span)[0:nc]


def stage_kernel(
    heads, span, side, nr, nc, in_ref, out_ref, up_ref, down_ref, weight_ref, ids_ref, mask_ref,
    chain_ref, in_out, out_out, up_out, down_out, weight_out, chain_out, row_mask, col_mask,
    ids_in, mask_in, chain_in, sems,
):
    lanes = heads * span
    copies = copies_of(
        (
            (ids_ref, ids_in), (mask_ref, mask_in), (chain_ref, chain_in), (in_ref, in_out),
            (out_ref, out_out), (up_ref, up_out), (down_ref, down_out), (weight_ref, weight_out),
        ),
        sems,
    )
    gr, gc = lax.axis_index("gr"), lax.axis_index("gc")
    for copy in copies[0:3]:
        copy.wait()
    ids = spread_ids(ids_in, lanes)
    chain_out[...] = chain_terms(
        ids, gc * nc, gr * nr, chain_weights(chain_in, 1, heads), heads, span
    )[0 : chain_out.shape[0]]
    mask = spread_ids(mask_in, lanes)
    row_mask[...] = key_mask(mask, gc, side, nc, lanes)
    col_mask[...] = key_mask(mask, gr, side, nr, lanes)
    for copy in copies[3:]:
        copy.wait()


def score_kernel(layer, heads, span, pieces, shape, *refs):
    nb, nt = shape
    in_ref, s_ref, v_ref, g_ref, base_ref, gather = refs[pieces:]
    width = base_ref.shape[1]
    length = pieces * nt
    weights = in_ref[layer]
    for k in range(pieces):
        value = refs[k][...].astype(F32)
        if value.ndim == 3:
            gather[:, k * nt : (k + 1) * nt, :] = value
        else:
            for b in range(nb):
                gather[b, k * nt : (k + 1) * nt, :] = value[b * nt : (b + 1) * nt]
    rows = base_ref.shape[0] // nb
    head_of = lax.broadcasted_iota(jnp.int32, (span, width), 1) // (width // heads)
    scale = LOG2E * (width // heads) ** (-0.5)
    step = nb // 2 if nb % 4 == 0 else nb
    for g in range(0, nb, step):
        exact = normal(gather[g : g + step].reshape(step * length, width))
        everyone = exact.astype(BF)
        part = slice(g * length, (g + step) * length)
        mine = jnp.concatenate(
            [everyone[b * length : b * length + span] for b in range(step)], axis=0
        )
        tight = jnp.concatenate([exact[b * length : b * length + rows] for b in range(step)], axis=0)
        some = slice(g * rows, (g + step) * rows)
        base_ref[some] = jnp.concatenate([gather[g + b, 0:rows, :] for b in range(step)], axis=0)
        query = jnp.dot(mine, weights[:, 0:width], preferred_element_type=F32).astype(BF)
        g_ref[some] = jnp.dot(
            tight.astype(BF), weights[:, 3 * width :], preferred_element_type=F32
        ).astype(BF)
        keys = jnp.dot(
            everyone, weights[:, width : 2 * width], preferred_element_type=F32
        ).astype(BF)
        v_ref[part] = jnp.dot(
            everyone, weights[:, 2 * width : 3 * width], preferred_element_type=F32
        ).astype(BF)
        for b in range(step):
            q = query[b * span : (b + 1) * span]
            wide = jnp.concatenate(
                [jnp.where(head_of == h, q, jnp.zeros_like(q)) for h in range(heads)], axis=0
            )
            s_ref[(g + b) * length : (g + b + 1) * length] = scale * contract(
                keys[b * length : (b + 1) * length], wide, 1, 1
            )


def attend(heads, span, pieces, s_ref, v_ref, g_ref, base_ref, bias_refs, mask_ref, out_w, table, probs):
    width = v_ref.shape[1]
    length = mask_ref.shape[0]
    nt = length // pieces
    nb = v_ref.shape[0] // length
    spin = lax.axis_index("gr") ^ lax.axis_index("gc")
    for slot in range(pieces):

        @pl.when(spin == slot)
        def _():
            for k in range(pieces):
                table[k * nt : (k + 1) * nt, :] = bias_refs[slot ^ k][...]

    shift = LOG2E * (table[...] + mask_ref[...])
    for b in range(nb):
        s = s_ref[b * length : (b + 1) * length] + shift
        e = jnp.exp2(s - jnp.max(s, axis=0, keepdims=True))
        probs[b * length : (b + 1) * length] = (
            e * (1.0 / jnp.sum(e, axis=0, keepdims=True))
        ).astype(BF)
    rows = base_ref.shape[0] // nb
    head_of = lax.broadcasted_iota(jnp.int32, (rows, width), 1) // (width // heads)
    done = []
    for group in range(GROUPS):
        mine = range(group * nb // GROUPS, (group + 1) * nb // GROUPS)
        mixed = []
        for b in mine:
            part = slice(b * length, (b + 1) * length)
            o = contract(probs[part], v_ref[part], 0, 0)
            got = o[0:rows]
            for h in range(1, heads):
                got = jnp.where(head_of == h, o[h * span : h * span + rows], got)
            mixed.append(got)
        part = slice(mine[0] * rows, (mine[-1] + 1) * rows)
        gate = jax.nn.sigmoid(g_ref[part].astype(F32))
        gated = (gate * jnp.concatenate(mixed, axis=0)).astype(BF)
        update = jnp.dot(gated, out_w, preferred_element_type=F32)
        done.append((base_ref[part] + update).astype(BF).astype(F32))
    return done


def first_kernel(heads, span, pieces, *refs):
    bias_refs = refs[4 : 4 + pieces]
    (
        mask_ref, out_ref, up_ref, down_ref, weight_ref, chain_ref,
        tile_ref, bias_ref, table, probs, turned,
    ) = refs[4 + pieces :]
    nb, _ = bias_ref.shape
    rows = tile_ref.shape[0] // nb
    done = attend(
        heads, span, pieces, *refs[0:4], bias_refs, mask_ref, out_ref[0], table, probs
    )
    parts = []
    for first in done:
        hidden = jnp.dot(norm32(first), up_ref[...], preferred_element_type=F32)
        hidden = jnp.maximum(hidden, 0.0).astype(BF)
        update = jnp.dot(hidden, down_ref[...], preferred_element_type=F32)
        parts.append((first + update).astype(BF).astype(F32))
    second = jnp.concatenate(parts, axis=0)
    tile_ref[...] = second
    nt = turned.shape[0] // rows
    turned[...] = jnp.zeros_like(turned)
    for b in range(nb):
        turned[pl.ds(b, nt, stride=rows), :] = second[b * rows : b * rows + nt]
    bias_ref[...] = select_terms(
        every_head(norm32(turned[...]), weight_ref[1], span), chain_ref[...], rows, nt, span
    )[0:nb]


def flip_kernel(nb, x_ref, o_ref, flip):
    rows = x_ref.shape[0] // nb
    nt = o_ref.shape[0] // nb
    for b in range(nb):
        flip[pl.ds(b, nt, stride=nb), :] = x_ref[b * rows : b * rows + nt]
    o_ref[...] = flip[...].astype(BF)


def second_kernel(heads, span, pieces, *refs):
    bias_refs = refs[4 : 4 + pieces]
    mask_ref, out_ref, tile_ref, table, probs, flip = refs[4 + pieces :]
    nt, nb, _ = tile_ref.shape
    done = attend(
        heads, span, pieces, *refs[0:4], bias_refs, mask_ref, out_ref[1], table, probs
    )
    last = jnp.concatenate(done, axis=0)
    rows = last.shape[0] // nb
    room = flip.shape[0] // nt
    for b in range(nb):
        flip[pl.ds(b, nt, stride=room), :] = last[b * rows : b * rows + nt]
    tile_ref[...] = flip[...].reshape(nt, room, -1)[:, 0:nb].astype(BF)


VMEM = pl.BlockSpec(memory_space=pltpu.VMEM)
SMEM = pl.BlockSpec(memory_space=pltpu.SMEM)
HBM = pl.BlockSpec(memory_space=pltpu.HBM)
PARAMS = pltpu.CompilerParams(vmem_limit_bytes=24 * 1024 * 1024)


def up_to_8(count):
    return -(-count // 8) * 8


def swap(array, axis, k):
    size = lax.axis_size(axis)
    return lax.ppermute(array, axis, [(i, i ^ k) for i in range(size)])


def scores(layer, heads, span, shape, chunks, weights):
    nb, nt = shape
    width = weights.shape[1]
    keys, own, lanes = nb * nt * len(chunks), nb * up_to_8(nt), heads * span
    return pl.pallas_call(
        functools.partial(score_kernel, layer, heads, span, len(chunks), shape),
        out_shape=(
            jax.ShapeDtypeStruct((keys, lanes), F32),
            jax.ShapeDtypeStruct((keys, width), BF),
            jax.ShapeDtypeStruct((own, width), BF),
            jax.ShapeDtypeStruct((own, width), F32),
        ),
        in_specs=[VMEM] * (len(chunks) + 1),
        out_specs=(VMEM,) * 4,
        scratch_shapes=[pltpu.VMEM((nb, len(chunks) * nt, width), F32)],
        compiler_params=PARAMS,
    )(*chunks, weights)


def fast_device(
    span, pair, mask, chain_ids, attn_in, attn_out, bias_weight, chain_bias, trans_up, trans_down
):
    side = lax.axis_size("gc")
    nr, nc, width = pair.shape
    heads = bias_weight.shape[2]
    lanes = heads * span
    cells = [(r, c) for r in range(side) for c in range(side)]
    weight = jnp.transpose(bias_weight, (0, 2, 1))
    ids, real = chain_ids[None, :], mask[None, :]

    def in_hbm(*arrays):
        return [pltpu.with_memory_space_constraint(a, pltpu.HBM) for a in arrays]

    def scratch_for(*arrays):
        return [pltpu.VMEM(a.shape, a.dtype) for a in arrays]

    far = swap(pair, "gc", 2)
    piece, own = pl.pallas_call(
        functools.partial(first_bias_kernel, heads, span),
        out_shape=(
            jax.ShapeDtypeStruct((nc, lanes), F32),
            jax.ShapeDtypeStruct((nr * nc, width), BF),
        ),
        in_specs=[HBM] * 4,
        out_specs=(VMEM,) * 2,
        scratch_shapes=[
            *scratch_for(pair),
            pltpu.VMEM((nr, up_to_8(nc), width), F32),
            pltpu.VMEM((nr * nc, width), F32),
            *scratch_for(weight, ids, chain_bias),
            pltpu.SemaphoreType.DMA((4,)),
        ],
        compiler_params=PARAMS,
    )(*in_hbm(pair, weight, ids, chain_bias))
    plain = (attn_in, attn_out, trans_up, trans_down, weight)
    small = (ids, real, chain_bias)
    attn_in, attn_out, trans_up, trans_down, weight, chain_two, row_mask, col_mask = (
        pl.pallas_call(
            functools.partial(stage_kernel, heads, span, side, nr, nc),
            out_shape=(
                *(jax.ShapeDtypeStruct(a.shape, a.dtype) for a in plain),
                jax.ShapeDtypeStruct((up_to_8(nr), lanes), F32),
                jax.ShapeDtypeStruct((side * nc, lanes), F32),
                jax.ShapeDtypeStruct((side * nr, lanes), F32),
            ),
            in_specs=[HBM] * 8,
            out_specs=(VMEM,) * 8,
            scratch_shapes=[*scratch_for(*small), pltpu.SemaphoreType.DMA((8,))],
            compiler_params=PARAMS,
        )(*in_hbm(*plain, *small))
    )
    pieces = [None] * side
    for k in FIRST_MOVES:
        got = lax.ppermute(
            piece, ("gr", "gc"), [(r * side + c, (c ^ k) * side + r) for r, c in cells]
        )
        pieces[k], pieces[k ^ 1] = got, swap(got, "gr", 1)
    last = swap(own, "gc", 3)
    near = swap(own, "gc", 1)
    heard = scores(0, heads, span, (nr, nc), [own, near, far, last], attn_in)
    second, piece = pl.pallas_call(
        functools.partial(first_kernel, heads, span, side),
        out_shape=(
            jax.ShapeDtypeStruct((nr * up_to_8(nc), width), F32),
            jax.ShapeDtypeStruct((nr, lanes), F32),
        ),
        in_specs=[VMEM] * (side + 10),
        out_specs=(VMEM, VMEM),
        scratch_shapes=[
            pltpu.VMEM((side * nc, lanes), F32),
            pltpu.VMEM((nr * side * nc, lanes), BF),
            pltpu.VMEM((nc * up_to_8(nr), width), F32),
        ],
        compiler_params=PARAMS,
    )(*heard, *pieces, row_mask, attn_out, trans_up, trans_down, weight, chain_two)
    tile = pl.pallas_call(
        functools.partial(flip_kernel, nr),
        out_shape=jax.ShapeDtypeStruct((nc * nr, width), BF),
        in_specs=[VMEM],
        out_specs=VMEM,
        scratch_shapes=[pltpu.VMEM((nc * nr, width), F32)],
        compiler_params=PARAMS,
    )(second)

    other = swap(piece, "gr", 1)
    chunks = [tile, swap(tile, "gr", 1)]
    for k in range(2, side, 2):
        far = swap(tile, "gr", k)
        chunks += [far, swap(far, "gr", 1)]
    both = jnp.stack([piece, other])
    pieces = [None] * side
    for k in LAST_MOVES:
        got = lax.ppermute(
            both, ("gr", "gc"), [(r * side + c, c * side + (r ^ k)) for r, c in cells]
        )
        pieces[k], pieces[k ^ 1] = got[0], got[1]
    heard = scores(1, heads, span, (nc, nr), chunks, attn_in)
    return pl.pallas_call(
        functools.partial(second_kernel, heads, span, side),
        out_shape=jax.ShapeDtypeStruct((nr, nc, width), BF),
        in_specs=[VMEM] * (side + 6),
        out_specs=VMEM,
        scratch_shapes=[
            pltpu.VMEM((side * nr, lanes), F32),
            pltpu.VMEM((nc * side * nr, lanes), BF),
            pltpu.VMEM((nr * up_to_8(nc), width), F32),
        ],
        compiler_params=PARAMS,
    )(*heard, *pieces, col_mask, attn_out)


FIRST_MOVES = (0, 2)
LAST_MOVES = (2, 1)


def solution(mesh):
    shape = dict(mesh.shape)
    in_specs = (P(("jobs", "gr"), "gc", None), P("jobs"), P("jobs"), P(), P(), P(), P(), P(), P())
    out_specs = P(("jobs", "gr"), "gc", None)
    side = shape["gc"]
    square = shape["gr"] == side and side == 4

    def per_device(*args):
        nr, nc, width = args[0].shape
        heads = args[5].shape[2]
        span = 128 // heads
        fits = nr == nc and nr <= span and (side * nr) % 16 == 0 and width == 128
        if square and fits:
            return fast_device(span, *args)
        return plain_device(*args)

    return jax.shard_map(
        per_device, mesh=mesh, in_specs=in_specs, out_specs=out_specs, check_vma=False
    )
```
